512 devices in a mesh: dp: 16 (over y, core), seq: 32 (over x, z).
Axes of the slice: x: 4, y: 8, z: 8, core: 2. Of those that a mesh axis runs over, the one named last changes fastest.
Arguments:
- queries: bfloat16 [16, 4096, 2048], P('dp', 'seq'), may hold values from -40 to 40, as said below
- keys: bfloat16 [16, 4096, 2048], P('dp', 'seq'), may hold values from -40 to 40, as said below
- values: bfloat16 [16, 4096, 2048], P('dp', 'seq'), may hold values from -40 to 40, as said below
- gain: float32 [2048], replicated, may hold values from 0.1 to 1.9
- cotangent: bfloat16 [16, 4096, 2048], P('dp', 'seq'), may hold values from -240 to 240, as said below
Outputs:
- output: bfloat16 [16, 4096, 2048], P('dp', 'seq')
- grad_query: bfloat16 [16, 4096, 2048], P('dp', 'seq')
- grad_key: bfloat16 [16, 4096, 2048], P('dp', 'seq')
- grad_value: bfloat16 [16, 4096, 2048], P('dp', 'seq')
- gain_grad: float32 [2048], replicated
The draws below stay inside these ranges and needn't reach their ends.
Inputs may be any that keep to these rules, and one draw needn't show every extreme that they name: queries: independent entries with row and feature scales. keys: independent entries with row and feature scales. values: independent entries with row and feature scales. cotangent: independent entries with row and feature scales.
All inputs are finite; a program needn't handle non-finite values.
Results may differ from the reference program's by a relative error of at most 0.0058.
Values may be sent and summed in bfloat16 or wider, within the bound.
A program may use at most 64 MiB of HBM per device.

```python
import jax
import jax.numpy as jnp
from jax import lax

HEADS = 16
HEAD = 128
TOK_DEV = 128
FEATURES = 2048
SEQS = 16
LEN = 4096
N_SEQ = 32


def rough_field(key, rising):
    shape = (SEQS, LEN, HEADS * HEAD)
    key_base, key_rows, key_cols = jax.random.split(key, 3)
    base = jnp.clip(jax.random.normal(key_base, shape, jnp.float32), -4.0, 4.0)
    top = 10.0
    slope = 2.0
    row_scale = jnp.exp(jax.random.uniform(key_rows, (SEQS, LEN, 1), jnp.float32) * jnp.log(top)) / jnp.sqrt(top)
    col_scale = jnp.exp(jax.random.uniform(key_cols, (1, 1, shape[2]), jnp.float32) * jnp.log(top)) / jnp.sqrt(top)
    field = base * row_scale * col_scale
    if rising:
        position = jnp.arange(LEN).astype(jnp.float32) / max(LEN - 1, 1)
        field = field * (1.0 + slope * position)[None, :, None]
    return field


def draw_queries(key, part):
    return rough_field(jax.random.fold_in(key, 101), False).astype(jnp.bfloat16)


def draw_keys(key, part):
    return rough_field(jax.random.fold_in(key, 202), False).astype(jnp.bfloat16)


def draw_values(key, part):
    return rough_field(jax.random.fold_in(key, 303), False).astype(jnp.bfloat16)


def draw_cotangent(key, part):
    return rough_field(jax.random.fold_in(key, 404), True).astype(jnp.bfloat16)


def setup_inputs(seed: int = 0) -> dict:
    arg_keys = jax.random.split(jax.random.key(seed), 6)
    queries = draw_queries(jax.random.fold_in(arg_keys[5], 71), 0)
    keys = draw_keys(jax.random.fold_in(arg_keys[5], 71), 0)
    values = draw_values(jax.random.fold_in(arg_keys[5], 71), 0)
    gain = jnp.clip(1.0 + 0.18 * jax.random.normal(arg_keys[3], (FEATURES,), jnp.float32), 0.1, 1.9)
    cotangent = draw_cotangent(jax.random.fold_in(arg_keys[5], 71), 0)
    return {"queries": queries, "keys": keys, "values": values, "gain": gain, "cotangent": cotangent}


EPSILON = 1e-06

def to_blocks(matrix):
    return matrix.astype(jnp.float32).reshape(N_SEQ, TOK_DEV, HEADS, HEAD)

def rounded(tensor):
    return lax.optimization_barrier(tensor.astype(jnp.bfloat16)).astype(jnp.float32)

def reference(queries, keys, values, gain, cotangent):
    scaling = HEAD ** (-0.5)
    position = jnp.arange(TOK_DEV)
    causal_mask = (position[:, None] >= position[None, :]).astype(jnp.float32)

    def one_sequence(operands):
        query_seq, key_seq, value_seq, upstream_seq = operands
        query_blocks = to_blocks(query_seq)
        key_blocks = to_blocks(key_seq)
        value_blocks = to_blocks(value_seq)
        local_states = jnp.einsum('bthd,bthe->bhde', key_blocks, value_blocks)
        prefix_states = jnp.concatenate([jnp.zeros_like(local_states[:1]), jnp.cumsum(local_states[:-1], axis=0)], axis=0)
        prefix_half = rounded(prefix_states)
        scores = jnp.einsum('bthd,buhd->bhtu', query_blocks, key_blocks) * scaling * causal_mask
        score_half = rounded(scores)
        attended = jnp.einsum('bhtu,buhe->bthe', score_half, value_blocks)
        attended = attended + scaling * jnp.einsum('bthd,bhde->bthe', query_blocks, prefix_half)
        attended = attended.reshape(LEN, HEADS * HEAD)
        root_mean = jnp.sqrt(lax.optimization_barrier(jnp.mean(attended * attended, axis=-1, keepdims=True)) + EPSILON)
        normalized = attended / root_mean
        output = (gain * normalized).astype(jnp.bfloat16)
        upstream = upstream_seq.astype(jnp.float32)
        gain_part = lax.optimization_barrier(jnp.sum(upstream * normalized, axis=0))
        scaled = upstream * gain
        inner_mean = lax.optimization_barrier(jnp.mean(scaled * normalized, axis=-1, keepdims=True))
        grad_attn = rounded((scaled - normalized * inner_mean) / root_mean)
        grad_blocks = grad_attn.reshape(N_SEQ, TOK_DEV, HEADS, HEAD)
        local_grads = scaling * jnp.einsum('bthd,bthe->bhde', query_blocks, grad_blocks)
        inclusive = jnp.cumsum(local_grads[::-1], axis=0)[::-1]
        suffix_states = jnp.concatenate([inclusive[1:], jnp.zeros_like(local_grads[:1])], axis=0)
        suffix_half = rounded(suffix_states)
        grad_scores = rounded(jnp.einsum('bthe,buhe->bhtu', grad_blocks, value_blocks) * causal_mask)
        grad_query = scaling * (jnp.einsum('bhtu,buhd->bthd', grad_scores, key_blocks) + jnp.einsum('bthe,bhde->bthd', grad_blocks, prefix_half))
        grad_key = scaling * jnp.einsum('bhtu,bthd->buhd', grad_scores, query_blocks) + jnp.einsum('buhe,bhde->buhd', value_blocks, suffix_half)
        grad_value = jnp.einsum('bhtu,bthe->buhe', score_half, grad_blocks) + jnp.einsum('buhd,bhde->buhe', key_blocks, suffix_half)
        shape_out = (LEN, HEADS * HEAD)
        return (output, grad_query.reshape(shape_out).astype(jnp.bfloat16), grad_key.reshape(shape_out).astype(jnp.bfloat16), grad_value.reshape(shape_out).astype(jnp.bfloat16), gain_part)
    results = lax.map(one_sequence, (queries, keys, values, cotangent))
    gain_grad = lax.optimization_barrier(jnp.sum(results[4], axis=0)) / SEQS
    return (results[0], results[1], results[2], results[3], gain_grad)
```

```python
import functools

import jax
import jax.numpy as jnp
from jax import lax
from jax.experimental import pallas as pl
from jax.experimental.pallas import tpu as pltpu
from jax.sharding import PartitionSpec as P

HEADS = 16
HEAD = 128
EPSILON = 1e-06
RING = 8
UNROLL = 4
MESH = pl.DeviceIdType.MESH
F32 = jnp.float32
BF16 = jnp.bfloat16


def dot(a, b, ca, cb):
    return lax.dot_general(a, b, (((ca,), (cb,)), ((), ())), preferred_element_type=F32)


def heads_loop(body):
    @pl.loop(0, HEADS // UNROLL)
    def _(step):
        for inner in range(UNROLL):
            body(step * UNROLL + inner)


def kernel(
    n_seq,
    n_dp,
    q_hbm,
    k_hbm,
    v_hbm,
    gain_hbm,
    cot_hbm,
    out_hbm,
    gq_hbm,
    gk_hbm,
    gv_hbm,
    gg_hbm,
    q_ref,
    k_ref,
    v_ref,
    cot_ref,
    gain_ref,
    att_ref,
    score_ref,
    ga_ref,
    gk_part,
    gv_part,
    out_ref,
    gq_ref,
    gk_ref,
    gv_ref,
    send_a,
    recv_a,
    send_b,
    recv_b,
    send_c,
    recv_c,
    send_d,
    recv_d,
    gain_part,
    gain_r1,
    gain_s2,
    gain_r2,
    gain_r3,
    gain_out,
    load_sem,
    store_sem,
    send_sem,
    recv_sem,
    gain_send_sem,
    gain_recv_sem,
    own_sem,
):
    seq = lax.axis_index("seq")
    dp = lax.axis_index("dp")
    rows = HEADS * HEAD // n_seq
    tokens = q_ref.shape[0]
    features = HEADS * HEAD
    scaling = HEAD ** (-0.5)
    n_x = n_seq // RING
    grows = HEADS // n_dp

    def slot(p):
        return pl.ds(pl.multiple_of(p * rows, rows), rows)

    def cols(h):
        return pl.ds(pl.multiple_of(h * HEAD, HEAD), HEAD)

    loads = [
        pltpu.make_async_copy(k_hbm.at[0], k_ref, load_sem.at[0]),
        pltpu.make_async_copy(v_hbm.at[0], v_ref, load_sem.at[1]),
        pltpu.make_async_copy(q_hbm.at[0], q_ref, load_sem.at[2]),
        pltpu.make_async_copy(cot_hbm.at[0], cot_ref, load_sem.at[3]),
        pltpu.make_async_copy(gain_hbm, gain_ref, load_sem.at[4]),
    ]
    for load in loads:
        load.start()

    barrier = pltpu.get_barrier_semaphore()

    @pl.loop(1, n_seq)
    def _(k):
        peer = lax.rem(seq + k, n_seq)
        pl.semaphore_signal(barrier, inc=1, device_id={"seq": peer}, device_id_type=MESH)

    @pl.loop(1, n_dp)
    def _(k):
        peer = lax.rem(dp + k, n_dp)
        pl.semaphore_signal(barrier, inc=1, device_id={"dp": peer}, device_id_type=MESH)

    def peer_at(k):
        j = k // n_x
        half = (j + 1) // 2
        offset = jnp.where(lax.rem(j, 2) == 0, RING // 2 + half, RING // 2 - half)
        step = lax.rem(lax.rem(k, n_x) + 1, n_x)
        z = lax.rem(lax.rem(seq, RING) + offset, RING)
        x = lax.rem(seq // RING + step, n_x)
        return x * RING + z

    def exchange(src, dst, index):
        @pl.loop(0, n_seq - 1)
        def _(k):
            peer = peer_at(k)
            pltpu.make_async_remote_copy(
                src_ref=src.at[slot(peer)],
                dst_ref=dst.at[slot(seq)],
                send_sem=send_sem.at[index],
                recv_sem=recv_sem.at[index],
                device_id={"seq": peer},
                device_id_type=MESH,
            ).start()

        own = pltpu.make_async_copy(src.at[slot(seq)], dst.at[slot(seq)], own_sem.at[index])
        own.start()
        return own

    def descriptor(src, dst, index):
        part = pl.ds(0, (n_seq - 1) * rows)
        return pltpu.make_async_remote_copy(
            src_ref=src.at[part],
            dst_ref=dst.at[part],
            send_sem=send_sem.at[index],
            recv_sem=recv_sem.at[index],
            device_id={"seq": lax.rem(seq + 1, n_seq)},
            device_id_type=MESH,
        )

    position_t = lax.broadcasted_iota(jnp.int32, (tokens, tokens), 0)
    position_u = lax.broadcasted_iota(jnp.int32, (tokens, tokens), 1)
    causal = position_t >= position_u

    loads[0].wait()
    loads[1].wait()

    def state_of(h):
        c = cols(h)
        send_a[c, :] = dot(k_ref[:, c], v_ref[:, c], 0, 0).astype(BF16)

    heads_loop(state_of)
    pl.semaphore_wait(barrier, n_seq - 1 + n_dp - 1)
    own_a = exchange(send_a, recv_a, 0)

    loads[2].wait()
    loads[3].wait()
    loads[4].wait()

    def local_of(h):
        c = cols(h)
        raw = dot(q_ref[:, c], k_ref[:, c], 1, 1)
        score = jnp.where(causal, raw * scaling, 0.0).astype(BF16)
        score_ref[c, :] = score
        att_ref[:, c] = dot(score, v_ref[:, c], 1, 0)

    heads_loop(local_of)

    def scan(src, dst, reverse):
        def step(i, total):
            b = n_seq - 1 - i if reverse else i
            dst[slot(b), :] = total.astype(BF16)
            return total + src[slot(b), :].astype(F32)

        lax.fori_loop(0, n_seq, step, jnp.zeros((rows, HEAD), F32))

    own_a.wait()
    descriptor(send_a, recv_a, 0).wait_recv()
    scan(recv_a, send_b, False)
    own_b = exchange(send_b, recv_b, 1)
    own_b.wait()
    descriptor(send_b, recv_b, 1).wait_recv()

    def attend(step, carry):
        squares, inner = carry
        for k in range(UNROLL):
            h = step * UNROLL + k
            c = cols(h)
            att = att_ref[:, c] + scaling * dot(q_ref[:, c], recv_b[c, :], 1, 0)
            att_ref[:, c] = att
            squares = squares + att * att
            inner = inner + att * (cot_ref[:, c].astype(F32) * gain_ref[pl.ds(h, 1), :])
        return squares, inner

    zero = jnp.zeros((tokens, HEAD), F32)
    squares, inner = lax.fori_loop(0, HEADS // UNROLL, attend, (zero, zero))
    root = jnp.sqrt(jnp.sum(squares, axis=1, keepdims=True) / features + EPSILON)
    inverse = 1.0 / root
    mean = jnp.sum(inner, axis=1, keepdims=True) * inverse / features

    def normalize(h):
        c = cols(h)
        weight = gain_ref[pl.ds(h, 1), :]
        upstream = cot_ref[:, c].astype(F32)
        normalized = att_ref[:, c] * inverse
        out_ref[:, c] = (weight * normalized).astype(BF16)
        gain_part[h] = jnp.sum(upstream * normalized, axis=0, keepdims=True)
        grad = ((upstream * weight - normalized * mean) * inverse).astype(BF16)
        ga_ref[:, c] = grad
        send_c[c, :] = (scaling * dot(q_ref[:, c], grad, 0, 0)).astype(BF16)

    heads_loop(normalize)
    own_c = exchange(send_c, recv_c, 2)

    def gain_copy(src, dst, index, axis, peer):
        return pltpu.make_async_remote_copy(
            src_ref=src,
            dst_ref=dst,
            send_sem=gain_send_sem.at[index],
            recv_sem=gain_recv_sem.at[index],
            device_id={axis: peer},
            device_id_type=MESH,
        )

    def part(j):
        return pl.ds(j * grows, grows)

    @pl.loop(1, n_dp)
    def _(k):
        peer = lax.rem(dp + k, n_dp)
        gain_copy(gain_part.at[part(peer)], gain_r1.at[part(dp)], 0, "dp", peer).start()

    store_out = pltpu.make_async_copy(out_ref, out_hbm.at[0], store_sem.at[0])
    store_out.start()

    def grads(h):
        c = cols(h)
        grad = ga_ref[:, c]
        gs = jnp.where(causal, dot(grad, v_ref[:, c], 1, 1), 0.0).astype(BF16)
        query = dot(gs, k_ref[:, c], 1, 0) + dot(grad, recv_b[c, :], 1, 1)
        gq_ref[:, c] = (scaling * query).astype(BF16)
        gk_part[:, c] = scaling * dot(gs, q_ref[:, c], 0, 0)
        gv_part[:, c] = dot(score_ref[c, :], grad, 0, 0)

    heads_loop(grads)
    store_gq = pltpu.make_async_copy(gq_ref, gq_hbm.at[0], store_sem.at[1])
    store_gq.start()

    gain_r1[part(dp)] = gain_part[part(dp)]
    others = pl.ds(0, (n_dp - 1) * grows)
    first = gain_copy(gain_part.at[others], gain_r1.at[others], 0, "dp", lax.rem(dp + 1, n_dp))
    first.wait_recv()
    summed = jnp.zeros((grows, 1, HEAD), F32)
    for j in range(n_dp):
        summed = summed + gain_r1[pl.ds(j * grows, grows)]
    gain_s2[...] = summed

    @pl.loop(0, n_seq - 1)
    def _(k):
        peer = peer_at(k)
        gain_copy(gain_s2, gain_r2.at[pl.ds(seq * grows, grows)], 1, "seq", peer).start()

    own_c.wait()
    descriptor(send_c, recv_c, 2).wait_recv()
    scan(recv_c, send_d, True)
    own_d = exchange(send_d, recv_d, 3)

    gain_r2[pl.ds(seq * grows, grows)] = summed
    some = pl.ds(0, (n_seq - 1) * grows)
    second = gain_copy(gain_r2.at[some], gain_r2.at[some], 1, "seq", lax.rem(seq + 1, n_seq))
    second.wait_recv()

    def add(j, total):
        return total + gain_r2[pl.ds(j * grows, grows)]

    total = lax.fori_loop(0, n_seq, add, jnp.zeros((grows, 1, HEAD), F32)) / n_dp
    gain_r3[part(dp)] = total

    @pl.loop(1, n_dp)
    def _(k):
        peer = lax.rem(dp + k, n_dp)
        gain_copy(gain_r3.at[part(dp)], gain_r3.at[part(dp)], 2, "dp", peer).start()

    own_d.wait()
    descriptor(send_d, recv_d, 3).wait_recv()

    def finish(h):
        c = cols(h)
        suffix = recv_d[c, :]
        gk_ref[:, c] = (gk_part[:, c] + dot(v_ref[:, c], suffix, 1, 1)).astype(BF16)
        gv_ref[:, c] = (gv_part[:, c] + dot(k_ref[:, c], suffix, 1, 0)).astype(BF16)

    heads_loop(finish)
    store_gk = pltpu.make_async_copy(gk_ref, gk_hbm.at[0], store_sem.at[2])
    store_gv = pltpu.make_async_copy(gv_ref, gv_hbm.at[0], store_sem.at[3])
    store_gk.start()
    store_gv.start()

    third = gain_copy(gain_r3.at[others], gain_r3.at[others], 2, "dp", lax.rem(dp + 1, n_dp))
    third.wait_recv()
    for h in range(HEADS):
        gain_out[h : h + 1, :] = gain_r3[h]
    store_gain = pltpu.make_async_copy(gain_out, gg_hbm, store_sem.at[4])
    store_gain.start()

    descriptor(send_a, recv_a, 0).wait_send()
    descriptor(send_b, recv_b, 1).wait_send()
    descriptor(send_c, recv_c, 2).wait_send()
    descriptor(send_d, recv_d, 3).wait_send()
    first.wait_send()
    second.wait_send()
    third.wait_send()
    for store in (store_out, store_gq, store_gk, store_gv, store_gain):
        store.wait()


def solution(mesh):
    n_seq = mesh.shape["seq"]
    n_dp = mesh.shape["dp"]

    def per_device(queries, keys, values, gain, cotangent):
        _, tokens, features = queries.shape
        grows = HEADS // n_dp
        exact = pltpu.VMEM((tokens, features), F32)
        half = pltpu.VMEM((tokens, features), BF16)
        states = pltpu.VMEM((features, HEAD), BF16)
        big = jax.ShapeDtypeStruct(queries.shape, BF16)
        anywhere = pl.BlockSpec(memory_space=pl.ANY)
        results = pl.pallas_call(
            functools.partial(kernel, n_seq, n_dp),
            out_shape=(big, big, big, big, jax.ShapeDtypeStruct((HEADS, HEAD), F32)),
            in_specs=[anywhere] * 5,
            out_specs=(anywhere,) * 5,
            scratch_shapes=[
                half,
                half,
                half,
                half,
                pltpu.VMEM((HEADS, HEAD), F32),
                exact,
                pltpu.VMEM((features, tokens), BF16),
                half,
                exact,
                exact,
                half,
                half,
                half,
                half,
            ]
            + [states] * 8
            + [
                pltpu.VMEM((HEADS, 1, HEAD), F32),
                pltpu.VMEM((HEADS, 1, HEAD), F32),
                pltpu.VMEM((grows, 1, HEAD), F32),
                pltpu.VMEM((n_seq * grows, 1, HEAD), F32),
                pltpu.VMEM((HEADS, 1, HEAD), F32),
                pltpu.VMEM((HEADS, HEAD), F32),
                pltpu.SemaphoreType.DMA((5,)),
                pltpu.SemaphoreType.DMA((5,)),
                pltpu.SemaphoreType.DMA((4,)),
                pltpu.SemaphoreType.DMA((4,)),
                pltpu.SemaphoreType.DMA((3,)),
                pltpu.SemaphoreType.DMA((3,)),
                pltpu.SemaphoreType.DMA((4,)),
            ],
            compiler_params=pltpu.CompilerParams(collective_id=0, has_side_effects=True),
        )(queries, keys, values, gain.reshape(HEADS, HEAD), cotangent)
        return (*results[:4], results[4].reshape(features))

    sharded = P("dp", "seq", None)
    return jax.shard_map(
        per_device,
        mesh=mesh,
        in_specs=(sharded, sharded, sharded, P(), sharded),
        out_specs=(sharded, sharded, sharded, sharded, P()),
        check_vma=False,
    )
```

```python
import functools

import jax
import jax.numpy as jnp
from jax import lax
from jax.experimental import pallas as pl
from jax.experimental.pallas import tpu as pltpu
from jax.sharding import PartitionSpec as P

HEADS = 16
HEAD = 128
EPSILON = 1e-06
RING = 8
CHUNKS = 2
ENTRIES = 6
MESH = pl.DeviceIdType.MESH
F32 = jnp.float32
BF16 = jnp.bfloat16


def dot(a, b, ca, cb):
    return lax.dot_general(a, b, (((ca,), (cb,)), ((), ())), preferred_element_type=F32)


class ScanPass:
    def __init__(self, index, reverse, refs, send_sem, recv_sem, n_x):
        self.state, self.child, self.group, self.inbox, self.outbox, self.back, self.down, self.result = refs
        self.index, self.reverse, self.n_x = index, reverse, n_x
        self.send_sem, self.recv_sem = send_sem, recv_sem
        seq = lax.axis_index("seq")
        self.x, self.z = seq // RING, lax.rem(seq, RING)
        self.share = HEAD // n_x

    def ring(self, offset):
        return lax.rem(self.z + (offset + RING), RING)

    def rows(self, start, size):
        return pl.ds(pl.multiple_of(start, self.share), size)

    def head(self, c, k):
        return self.rows((c * CHUNKS + k) * HEAD, HEAD)

    def piece(self, c, k, x):
        return self.rows((c * CHUNKS + k) * HEAD + x * self.share, self.share)

    def spot(self, k, x, entry):
        return self.rows(((k * self.n_x + x) * ENTRIES + entry) * self.share, self.share)

    def tile(self, k, i, count):
        return self.rows((k * count + i) * HEAD, HEAD)

    def tile_part(self, k, i, count, x):
        return self.rows((k * count + i) * HEAD + x * self.share, self.share)

    def copy(self, src, dst, k, send, recv, x, z):
        return pltpu.make_async_remote_copy(
            src_ref=src,
            dst_ref=dst,
            send_sem=self.send_sem.at[self.index, k, send],
            recv_sem=self.recv_sem.at[self.index, k, recv],
            device_id={"seq": x * RING + z},
            device_id_type=MESH,
        )

    def taken(self, count, k, kind):
        part = pl.ds(0, count * self.share)
        return self.copy(self.state.at[part], self.result.at[part], k, kind, kind, self.x, self.ring(1))

    def inner(self):
        return jnp.logical_and(self.z >= 2, self.z <= 5)

    def clear(self):
        zero = jnp.zeros((HEAD, HEAD), BF16)
        few = jnp.zeros((self.share, HEAD), BF16)
        z = self.z

        @pl.when(z == 0)
        def _():
            for k in range(CHUNKS):
                self.child[self.tile(k, 0, 4), :] = zero

        @pl.when(z == RING - 1)
        def _():
            for k in range(CHUNKS):
                self.child[self.tile(k, 2, 4), :] = zero

        @pl.when(jnp.logical_not(self.inner()))
        def _():
            for k in range(CHUNKS):
                self.child[self.tile(k, 1, 4), :] = zero
                self.child[self.tile(k, 3, 4), :] = zero

        @pl.when(jnp.logical_not(jnp.logical_or(z == 2, z == 5)))
        def _():
            for k in range(CHUNKS):
                for x in range(self.n_x):
                    self.inbox[self.spot(k, x, 0), :] = few

    def send_far(self, k):
        z = self.z

        def hand(offset, to, slot, send):
            self.copy(
                self.state.at[self.head(self.ring(offset), k)],
                self.child.at[self.tile(k, slot, 4)],
                k,
                send,
                slot,
                self.x,
                to,
            ).start()

        pl.when(z < 4)(lambda: hand(4, z + 2, 1, 2))
        pl.when(z >= 4)(lambda: hand(4, z - 2, 3, 2))
        pl.when(z != RING - 1)(lambda: hand(3, z + 1, 0, 0))
        pl.when(z != 0)(lambda: hand(-3, z - 1, 2, 1))

    def send_near(self, k):
        z, n_x = self.z, self.n_x

        def direct(c, x, entry, kind):
            self.copy(
                self.state.at[self.piece(c, k, x)], self.inbox.at[self.spot(k, self.x, entry)], k, kind, kind, x, c
            ).start()

        for i in range(n_x):
            x = lax.rem(self.x + (i + 1), n_x)
            pl.when(z == RING - 1)(functools.partial(direct, 2, x, 0, 5))
            pl.when(z == 0)(functools.partial(direct, 5, x, 0, 5))
            direct(self.ring(1), x, 2, 4)
            direct(self.ring(-1), x, 4, 4)
            if i < n_x - 1:
                direct(z, x, 3, 4)
        self.inbox[self.spot(k, self.x, 3), :] = self.state[self.piece(z, k, self.x), :]

    def relay(self, k):
        z, n_x = self.z, self.n_x
        whole = n_x
        pl.when(z != 0)(lambda: self.taken(whole, k, 0).wait_recv())
        pl.when(z != RING - 1)(lambda: self.taken(whole, k, 2).wait_recv())

        @pl.when(self.inner())
        def _():
            self.taken(whole, k, 1).wait_recv()
            self.taken(whole, k, 3).wait_recv()

        for side in range(2):
            c = self.ring(2 - 4 * side)
            total = self.state[self.head(c, k), :].astype(F32)
            total = total + self.child[self.tile(k, 2 * side, 4), :].astype(F32)
            total = total + self.child[self.tile(k, 2 * side + 1, 4), :].astype(F32)
            self.group[self.tile(k, side, 2), :] = total.astype(BF16)
        for i in range(n_x):
            x = lax.rem(self.x + (i + 1), n_x)
            for side in range(2):
                self.copy(
                    self.group.at[self.tile_part(k, side, 2, x)],
                    self.inbox.at[self.spot(k, self.x, 1 + 4 * side)],
                    k,
                    4,
                    4,
                    x,
                    self.ring(2 - 4 * side),
                ).start()

    def own(self, k):
        z, n_x = self.z, self.n_x
        pl.when(jnp.logical_or(z == 2, z == 5))(lambda: self.taken(n_x, k, 5).wait_recv())
        self.taken(5 * n_x - 1, k, 4).wait_recv()
        first = jnp.where(z <= 3, 3 - z, jnp.where(z <= 5, 0, 11 - z))
        total = jnp.zeros((self.share, HEAD), F32)
        for i in range(n_x * ENTRIES):
            j = n_x * ENTRIES - 1 - i if self.reverse else i
            spot = self.spot(k, j // ENTRIES, lax.rem(first + j % ENTRIES, ENTRIES))
            self.outbox[spot, :] = total.astype(BF16)
            total = total + self.inbox[spot, :].astype(F32)

        def give(x, to, entry, kind):
            self.copy(
                self.outbox.at[self.spot(k, x, entry)], self.result.at[self.piece(z, k, self.x)], k, kind, kind, x, to
            ).start()

        def give_group(x, side):
            self.copy(
                self.outbox.at[self.spot(k, x, 1 + 4 * side)],
                self.back.at[self.tile_part(k, side, 2, self.x)],
                k,
                6,
                8 + side,
                x,
                self.ring(4 * side - 2),
            ).start()

        for i in range(n_x):
            x = lax.rem(self.x + (i + 1), n_x)
            give_group(x, 0)
            give_group(x, 1)
        for i in range(n_x):
            x = lax.rem(self.x + (i + 1), n_x)
            pl.when(z == 2)(functools.partial(give, x, RING - 1, 0, 7))
            pl.when(z == 5)(functools.partial(give, x, 0, 0, 7))
            give(x, self.ring(-1), 2, 6)
            give(x, self.ring(1), 4, 6)
            if i < n_x - 1:
                give(x, z, 3, 6)
        self.result[self.piece(z, k, self.x), :] = self.outbox[self.spot(k, self.x, 3), :]

    def pass_on(self, k):
        z = self.z
        for side in range(2):
            c = self.ring(2 - 4 * side)
            self.taken(self.n_x, k, 8 + side).wait_recv()
            base = self.back[self.tile(k, side, 2), :].astype(F32)
            mine = self.state[self.head(c, k), :].astype(F32)
            near = self.child[self.tile(k, 2 * side, 4), :].astype(F32)
            far = self.child[self.tile(k, 2 * side + 1, 4), :].astype(F32)
            if (side == 0) != self.reverse:
                for_far = base
                for_near = base + far
                for_mine = for_near + near
            else:
                for_mine = base
                for_near = base + mine
                for_far = for_near + near
            self.down[self.tile(k, 2 * side + 1, 4), :] = for_far.astype(BF16)
            self.down[self.tile(k, 2 * side, 4), :] = for_near.astype(BF16)
            self.result[self.head(c, k), :] = for_mine.astype(BF16)

        def hand(side, slot, to, send, recv):
            self.copy(
                self.down.at[self.tile(k, slot, 4)],
                self.result.at[self.head(self.ring(2 - 4 * side), k)],
                k,
                send,
                recv,
                self.x,
                to,
            ).start()

        @pl.when(self.inner())
        def _():
            hand(0, 1, z - 2, 10, 12)
            hand(1, 3, z + 2, 11, 12)

        pl.when(z != 0)(lambda: hand(0, 0, z - 1, 8, 10))
        pl.when(z != RING - 1)(lambda: hand(1, 2, z + 1, 9, 11))

    def arrive(self, k):
        z, n_x = self.z, self.n_x
        self.taken(3 * n_x - 1, k, 6).wait_recv()
        pl.when(jnp.logical_or(z == 0, z == RING - 1))(lambda: self.taken(n_x, k, 7).wait_recv())
        pl.when(z != RING - 1)(lambda: self.taken(n_x, k, 10).wait_recv())
        pl.when(z != 0)(lambda: self.taken(n_x, k, 11).wait_recv())
        self.taken(n_x, k, 12).wait_recv()

    def drain(self, k):
        z, n_x = self.z, self.n_x

        def sent(count, kind):
            self.taken(count, k, kind).wait_send()

        pl.when(z != RING - 1)(lambda: sent(n_x, 0))
        pl.when(z != 0)(lambda: sent(n_x, 1))
        sent(n_x, 2)
        sent(5 * n_x - 1, 4)
        pl.when(jnp.logical_or(z == 0, z == RING - 1))(lambda: sent(n_x, 5))
        sent(5 * n_x - 1, 6)
        pl.when(jnp.logical_or(z == 2, z == 5))(lambda: sent(n_x, 7))
        pl.when(z != 0)(lambda: sent(n_x, 8))
        pl.when(z != RING - 1)(lambda: sent(n_x, 9))

        @pl.when(self.inner())
        def _():
            sent(n_x, 10)
            sent(n_x, 11)


PASS_REFS = 8
KINDS = 13


def pass_scratch(n_x):
    tiles = CHUNKS * HEAD
    sizes = (
        HEADS * HEAD,
        4 * tiles,
        2 * tiles,
        ENTRIES * tiles,
        ENTRIES * tiles,
        2 * tiles,
        4 * tiles,
        HEADS * HEAD,
    )
    return [pltpu.VMEM((size, HEAD), BF16) for size in sizes]


def chunk_loop(k, body):
    @pl.loop(0, HEADS // CHUNKS // 4)
    def _(step):
        for inner in range(4):
            body((step * 4 + inner) * CHUNKS + k)


def kernel(
    n_seq,
    n_dp,
    q_hbm,
    k_hbm,
    v_hbm,
    gain_hbm,
    cot_hbm,
    out_hbm,
    gq_hbm,
    gk_hbm,
    gv_hbm,
    gg_hbm,
    q_ref,
    k_ref,
    v_ref,
    cot_ref,
    gain_ref,
    att_ref,
    score_ref,
    ga_ref,
    gk_part,
    gv_part,
    out_ref,
    gq_ref,
    gk_ref,
    gv_ref,
    *rest,
):
    ahead_refs, rest = rest[:PASS_REFS], rest[PASS_REFS:]
    behind_refs, rest = rest[:PASS_REFS], rest[PASS_REFS:]
    gain_part, gain_r1, gain_s2, gain_r2, gain_r3, gain_out, *sems = rest
    load_sem, store_sem, send_sem, recv_sem, gain_send_sem, gain_recv_sem = sems
    seq = lax.axis_index("seq")
    dp = lax.axis_index("dp")
    n_x = n_seq // RING
    ahead = ScanPass(0, False, ahead_refs, send_sem, recv_sem, n_x)
    behind = ScanPass(1, True, behind_refs, send_sem, recv_sem, n_x)
    tokens = q_ref.shape[0]
    features = HEADS * HEAD
    scaling = HEAD ** (-0.5)
    grows = HEADS // n_dp

    def cols(h):
        return pl.ds(pl.multiple_of(h * HEAD, HEAD), HEAD)

    loads = [
        pltpu.make_async_copy(k_hbm.at[0], k_ref, load_sem.at[0]),
        pltpu.make_async_copy(v_hbm.at[0], v_ref, load_sem.at[1]),
        pltpu.make_async_copy(q_hbm.at[0], q_ref, load_sem.at[2]),
        pltpu.make_async_copy(cot_hbm.at[0], cot_ref, load_sem.at[3]),
        pltpu.make_async_copy(gain_hbm, gain_ref, load_sem.at[4]),
    ]
    for load in loads:
        load.start()

    barrier = pltpu.get_barrier_semaphore()

    @pl.loop(1, n_seq)
    def _(k):
        peer = lax.rem(seq + k, n_seq)
        pl.semaphore_signal(barrier, inc=1, device_id={"seq": peer}, device_id_type=MESH)

    @pl.loop(1, n_dp)
    def _(k):
        peer = lax.rem(dp + k, n_dp)
        pl.semaphore_signal(barrier, inc=1, device_id={"dp": peer}, device_id_type=MESH)

    ahead.clear()
    behind.clear()

    position_t = lax.broadcasted_iota(jnp.int32, (tokens, tokens), 0)
    position_u = lax.broadcasted_iota(jnp.int32, (tokens, tokens), 1)
    causal = position_t >= position_u

    loads[0].wait()
    loads[1].wait()

    def state_of(h):
        c = cols(h)
        ahead.state[c, :] = dot(k_ref[:, c], v_ref[:, c], 0, 0).astype(BF16)

    chunk_loop(0, state_of)
    pl.semaphore_wait(barrier, n_seq - 1 + n_dp - 1)
    ahead.send_far(0)
    chunk_loop(1, state_of)
    ahead.send_far(1)
    ahead.send_near(0)
    ahead.send_near(1)

    loads[2].wait()
    loads[3].wait()
    loads[4].wait()

    def local_of(h):
        c = cols(h)
        raw = dot(q_ref[:, c], k_ref[:, c], 1, 1)
        score = jnp.where(causal, raw * scaling, 0.0).astype(BF16)
        score_ref[c, :] = score
        att_ref[:, c] = dot(score, v_ref[:, c], 1, 0)

    chunk_loop(0, local_of)
    ahead.relay(0)
    ahead.relay(1)
    chunk_loop(1, local_of)
    ahead.own(0)
    ahead.own(1)
    ahead.pass_on(0)
    ahead.pass_on(1)

    def attend(chunk, step, carry):
        squares, inner = carry
        for k in range(4):
            h = (step * 4 + k) * CHUNKS + chunk
            c = cols(h)
            att = att_ref[:, c] + scaling * dot(q_ref[:, c], ahead.result[c, :], 1, 0)
            att_ref[:, c] = att
            squares = squares + att * att
            inner = inner + att * (cot_ref[:, c].astype(F32) * gain_ref[pl.ds(h, 1), :])
        return squares, inner

    zero = jnp.zeros((tokens, HEAD), F32)
    carry = (zero, zero)
    for chunk in range(CHUNKS):
        ahead.arrive(chunk)
        carry = lax.fori_loop(0, HEADS // CHUNKS // 4, functools.partial(attend, chunk), carry)
    squares, inner = carry
    root = jnp.sqrt(jnp.sum(squares, axis=1, keepdims=True) / features + EPSILON)
    inverse = 1.0 / root
    mean = jnp.sum(inner, axis=1, keepdims=True) * inverse / features

    def normalize(h):
        c = cols(h)
        weight = gain_ref[pl.ds(h, 1), :]
        upstream = cot_ref[:, c].astype(F32)
        normalized = att_ref[:, c] * inverse
        out_ref[:, c] = (weight * normalized).astype(BF16)
        gain_part[h] = jnp.sum(upstream * normalized, axis=0, keepdims=True)
        grad = ((upstream * weight - normalized * mean) * inverse).astype(BF16)
        ga_ref[:, c] = grad
        behind.state[c, :] = (scaling * dot(q_ref[:, c], grad, 0, 0)).astype(BF16)

    chunk_loop(0, normalize)
    behind.send_far(0)
    chunk_loop(1, normalize)
    behind.send_far(1)
    behind.send_near(0)
    behind.send_near(1)

    def gain_copy(src, dst, index, axis, peer):
        return pltpu.make_async_remote_copy(
            src_ref=src,
            dst_ref=dst,
            send_sem=gain_send_sem.at[index],
            recv_sem=gain_recv_sem.at[index],
            device_id={axis: peer},
            device_id_type=MESH,
        )

    def part(j):
        return pl.ds(j * grows, grows)

    @pl.loop(1, n_dp)
    def _(k):
        peer = lax.rem(dp + k, n_dp)
        gain_copy(gain_part.at[part(peer)], gain_r1.at[part(dp)], 0, "dp", peer).start()

    store_out = pltpu.make_async_copy(out_ref, out_hbm.at[0], store_sem.at[0])
    store_out.start()

    def grads(h):
        c = cols(h)
        grad = ga_ref[:, c]
        gs = jnp.where(causal, dot(grad, v_ref[:, c], 1, 1), 0.0).astype(BF16)
        query = dot(gs, k_ref[:, c], 1, 0) + dot(grad, ahead.result[c, :], 1, 1)
        gq_ref[:, c] = (scaling * query).astype(BF16)
        gk_part[:, c] = scaling * dot(gs, q_ref[:, c], 0, 0)
        gv_part[:, c] = dot(score_ref[c, :], grad, 0, 0)

    chunk_loop(0, grads)
    behind.relay(0)
    behind.relay(1)
    chunk_loop(1, grads)
    store_gq = pltpu.make_async_copy(gq_ref, gq_hbm.at[0], store_sem.at[1])
    store_gq.start()

    gain_r1[part(dp)] = gain_part[part(dp)]
    others = pl.ds(0, (n_dp - 1) * grows)
    first = gain_copy(gain_part.at[others], gain_r1.at[others], 0, "dp", lax.rem(dp + 1, n_dp))
    first.wait_recv()
    summed = jnp.zeros((grows, 1, HEAD), F32)
    for j in range(n_dp):
        summed = summed + gain_r1[pl.ds(j * grows, grows)]
    gain_s2[...] = summed

    @pl.loop(1, n_seq)
    def _(k):
        peer = lax.rem(seq + k, n_seq)
        gain_copy(gain_s2, gain_r2.at[pl.ds(seq * grows, grows)], 1, "seq", peer).start()

    behind.own(0)
    behind.own(1)

    behind.pass_on(0)
    behind.pass_on(1)

    gain_r2[pl.ds(seq * grows, grows)] = summed
    some = pl.ds(0, (n_seq - 1) * grows)
    second = gain_copy(gain_r2.at[some], gain_r2.at[some], 1, "seq", lax.rem(seq + 1, n_seq))
    second.wait_recv()

    def add(j, total):
        return total + gain_r2[pl.ds(j * grows, grows)]

    total = lax.fori_loop(0, n_seq, add, jnp.zeros((grows, 1, HEAD), F32)) / n_dp
    gain_r3[part(dp)] = total

    @pl.loop(1, n_dp)
    def _(k):
        peer = lax.rem(dp + k, n_dp)
        gain_copy(gain_r3.at[part(dp)], gain_r3.at[part(dp)], 2, "dp", peer).start()


    def finish(h):
        c = cols(h)
        suffix = behind.result[c, :]
        gk_ref[:, c] = (gk_part[:, c] + dot(v_ref[:, c], suffix, 1, 1)).astype(BF16)
        gv_ref[:, c] = (gv_part[:, c] + dot(k_ref[:, c], suffix, 1, 0)).astype(BF16)

    for chunk in range(CHUNKS):
        behind.arrive(chunk)
        chunk_loop(chunk, finish)
    store_gk = pltpu.make_async_copy(gk_ref, gk_hbm.at[0], store_sem.at[2])
    store_gv = pltpu.make_async_copy(gv_ref, gv_hbm.at[0], store_sem.at[3])
    store_gk.start()
    store_gv.start()

    third = gain_copy(gain_r3.at[others], gain_r3.at[others], 2, "dp", lax.rem(dp + 1, n_dp))
    third.wait_recv()
    for h in range(HEADS):
        gain_out[h : h + 1, :] = gain_r3[h]
    store_gain = pltpu.make_async_copy(gain_out, gg_hbm, store_sem.at[4])
    store_gain.start()

    for chunk in range(CHUNKS):
        ahead.drain(chunk)
        behind.drain(chunk)
    first.wait_send()
    second.wait_send()
    third.wait_send()
    for store in (store_out, store_gq, store_gk, store_gv, store_gain):
        store.wait()


def hand_out(*refs):
    sources, targets, sem = refs[:5], refs[5:10], refs[10]
    stores = [pltpu.make_async_copy(a, b, sem.at[i]) for i, (a, b) in enumerate(zip(sources, targets))]
    for store in stores:
        store.start()
    for store in stores:
        store.wait()


def stay(array):
    return pltpu.with_memory_space_constraint(array, pltpu.HBM)


def solution(mesh):
    n_seq = mesh.shape["seq"]
    n_dp = mesh.shape["dp"]

    def per_device(queries, keys, values, gain, cotangent):
        _, tokens, features = queries.shape
        grows = HEADS // n_dp
        exact = pltpu.VMEM((tokens, features), F32)
        half = pltpu.VMEM((tokens, features), BF16)
        big = jax.ShapeDtypeStruct(queries.shape, BF16)
        anywhere = pl.BlockSpec(memory_space=pl.ANY)
        results = pl.pallas_call(
            functools.partial(kernel, n_seq, n_dp),
            out_shape=(big, big, big, big, jax.ShapeDtypeStruct((HEADS, HEAD), F32)),
            in_specs=[pl.BlockSpec(memory_space=pltpu.HBM)] * 5,
            out_specs=(anywhere,) * 5,
            scratch_shapes=[
                half,
                half,
                half,
                half,
                pltpu.VMEM((HEADS, HEAD), F32),
                exact,
                pltpu.VMEM((features, tokens), BF16),
                half,
                exact,
                exact,
                half,
                half,
                half,
                half,
            ]
            + pass_scratch(n_seq // RING) * 2
            + [
                pltpu.VMEM((HEADS, 1, HEAD), F32),
                pltpu.VMEM((HEADS, 1, HEAD), F32),
                pltpu.VMEM((grows, 1, HEAD), F32),
                pltpu.VMEM((n_seq * grows, 1, HEAD), F32),
                pltpu.VMEM((HEADS, 1, HEAD), F32),
                pltpu.VMEM((HEADS, HEAD), F32),
                pltpu.SemaphoreType.DMA((5,)),
                pltpu.SemaphoreType.DMA((5,)),
                pltpu.SemaphoreType.DMA((2, CHUNKS, KINDS)),
                pltpu.SemaphoreType.DMA((2, CHUNKS, KINDS)),
                pltpu.SemaphoreType.DMA((3,)),
                pltpu.SemaphoreType.DMA((3,)),
            ],
            compiler_params=pltpu.CompilerParams(
                collective_id=0, has_side_effects=True, vmem_limit_bytes=32 * 2**20
            ),
        )(*(stay(a) for a in (queries, keys, values, gain.reshape(HEADS, HEAD), cotangent)))
        small = jax.ShapeDtypeStruct((HEADS, HEAD), F32)
        results = pl.pallas_call(
            hand_out,
            out_shape=(big, big, big, big, small),
            in_specs=[anywhere] * 5,
            out_specs=(anywhere,) * 5,
            scratch_shapes=[pltpu.SemaphoreType.DMA((5,))],
            compiler_params=pltpu.CompilerParams(vmem_limit_bytes=2**20),
        )(*results)
        return (*results[:4], results[4].reshape(features))

    sharded = P("dp", "seq", None)
    return jax.shard_map(
        per_device,
        mesh=mesh,
        in_specs=(sharded, sharded, sharded, P(), sharded),
        out_specs=(sharded, sharded, sharded, sharded, P()),
        check_vma=False,
    )
```

```python
import functools

import jax
import jax.numpy as jnp
from jax import lax
from jax.experimental import pallas as pl
from jax.experimental.pallas import tpu as pltpu
from jax.sharding import PartitionSpec as P

HEADS = 16
HEAD = 128
EPSILON = 1e-06
RING = 8
CHUNKS = 2
ENTRIES = 6
MESH = pl.DeviceIdType.MESH
F32 = jnp.float32
BF16 = jnp.bfloat16


def dot(a, b, ca, cb):
    return lax.dot_general(a, b, (((ca,), (cb,)), ((), ())), preferred_element_type=F32)


class ScanPass:
    def __init__(self, index, reverse, refs, send_sem, recv_sem, n_x):
        self.state, self.child, self.group, self.inbox, self.outbox, self.back, self.down, self.result = refs
        self.index, self.reverse, self.n_x = index, reverse, n_x
        self.send_sem, self.recv_sem = send_sem, recv_sem
        seq = lax.axis_index("seq")
        self.x, self.z = seq // RING, lax.rem(seq, RING)
        self.share = HEAD // n_x

    def ring(self, offset):
        return lax.rem(self.z + (offset + RING), RING)

    def rows(self, start, size):
        return pl.ds(pl.multiple_of(start, self.share), size)

    def head(self, c, k):
        return self.rows((c * CHUNKS + k) * HEAD, HEAD)

    def piece(self, c, k, x):
        return self.rows((c * CHUNKS + k) * HEAD + x * self.share, self.share)

    def spot(self, k, x, entry):
        return self.rows(((k * self.n_x + x) * ENTRIES + entry) * self.share, self.share)

    def tile(self, k, i, count):
        return self.rows((k * count + i) * HEAD, HEAD)

    def tile_part(self, k, i, count, x):
        return self.rows((k * count + i) * HEAD + x * self.share, self.share)

    def copy(self, src, dst, k, send, recv, x, z):
        return pltpu.make_async_remote_copy(
            src_ref=src,
            dst_ref=dst,
            send_sem=self.send_sem.at[self.index, k, send],
            recv_sem=self.recv_sem.at[self.index, k, recv],
            device_id={"seq": x * RING + z},
            device_id_type=MESH,
        )

    def taken(self, count, k, kind):
        part = pl.ds(0, count * self.share)
        return self.copy(self.state.at[part], self.result.at[part], k, kind, kind, self.x, self.ring(1))

    def odd(self):
        return jnp.logical_or(self.z == 0, self.z == RING - 1)

    def even_inner(self):
        return jnp.logical_and(self.z != 0, lax.rem(self.z, 2) == 0)

    def odd_inner(self):
        return jnp.logical_and(self.z != RING - 1, lax.rem(self.z, 2) == 1)

    def odd_owner(self):
        return jnp.logical_or(self.z == 2, self.z == 5)

    def odd_target(self):
        return jnp.where(self.z == 0, 5, 2)

    def clear(self):
        zero = jnp.zeros((HEAD, HEAD), BF16)
        few = jnp.zeros((self.share, HEAD), BF16)

        def blank(slot):
            for k in range(CHUNKS):
                self.child[self.tile(k, slot, 5), :] = zero

        pl.when(self.z == 0)(lambda: blank(0))
        pl.when(self.z == RING - 1)(lambda: blank(2))
        pl.when(jnp.logical_not(self.even_inner()))(lambda: blank(1))
        pl.when(jnp.logical_not(self.odd_inner()))(lambda: blank(3))

        @pl.when(jnp.logical_not(self.odd_owner()))
        def _():
            for k in range(CHUNKS):
                for x in range(self.n_x):
                    self.inbox[self.spot(k, x, 0), :] = few

    def send_far(self, k):
        z = self.z

        def hand(offset, to, slot, send):
            self.copy(
                self.state.at[self.head(self.ring(offset), k)],
                self.child.at[self.tile(k, slot, 5)],
                k,
                send,
                slot if slot < 4 else 13,
                self.x,
                to,
            ).start()

        even = lax.rem(z, 2) == 0
        pl.when(jnp.logical_and(even, z != 6))(lambda: hand(4, z + 2, 1, 2))
        pl.when(jnp.logical_not(jnp.logical_or(even, z == 1)))(lambda: hand(4, z - 2, 3, 2))
        pl.when(z == 6)(lambda: hand(4, z + 1, 4, 2))
        pl.when(z == 1)(lambda: hand(4, z - 1, 4, 2))
        pl.when(z != RING - 1)(lambda: hand(3, z + 1, 0, 0))
        pl.when(z != 0)(lambda: hand(-3, z - 1, 2, 1))

    def send_near(self, k):
        z, n_x = self.z, self.n_x

        def direct(c, x, entry, kind):
            self.copy(
                self.state.at[self.piece(c, k, x)], self.inbox.at[self.spot(k, self.x, entry)], k, kind, kind, x, c
            ).start()

        for i in range(n_x):
            x = lax.rem(self.x + (i + 1), n_x)
            direct(self.ring(1), x, 2, 4)
            direct(self.ring(-1), x, 4, 4)
            if i < n_x - 1:
                direct(z, x, 3, 4)
        self.inbox[self.spot(k, self.x, 3), :] = self.state[self.piece(z, k, self.x), :]

    def relay(self, k):
        z, n_x = self.z, self.n_x
        whole = n_x
        for side in range(2):
            if side == 0:
                pl.when(z != 0)(lambda: self.taken(whole, k, 0).wait_recv())
                pl.when(self.even_inner())(lambda: self.taken(whole, k, 1).wait_recv())
            else:
                pl.when(z != RING - 1)(lambda: self.taken(whole, k, 2).wait_recv())
                pl.when(self.odd_inner())(lambda: self.taken(whole, k, 3).wait_recv())
            c = self.ring(2 - 4 * side)
            total = self.state[self.head(c, k), :].astype(F32)
            total = total + self.child[self.tile(k, 2 * side, 5), :].astype(F32)
            total = total + self.child[self.tile(k, 2 * side + 1, 5), :].astype(F32)
            self.group[self.tile(k, side, 3), :] = total.astype(BF16)
            for i in range(n_x):
                x = lax.rem(self.x + (i + 1), n_x)
                self.copy(
                    self.group.at[self.tile_part(k, side, 3, x)],
                    self.inbox.at[self.spot(k, self.x, 1 + 4 * side)],
                    k,
                    4,
                    4,
                    x,
                    c,
                ).start()

        @pl.when(self.odd())
        def _():
            self.taken(whole, k, 13).wait_recv()
            c = self.odd_target()
            total = self.state[self.head(c, k), :].astype(F32) + self.child[self.tile(k, 4, 5), :].astype(F32)
            self.group[self.tile(k, 2, 3), :] = total.astype(BF16)
            for i in range(n_x):
                x = lax.rem(self.x + (i + 1), n_x)
                source = self.group.at[self.tile_part(k, 2, 3, x)]
                self.copy(source, self.inbox.at[self.spot(k, self.x, 0)], k, 5, 5, x, c).start()

    def own(self, k):
        z, n_x = self.z, self.n_x
        pl.when(self.odd_owner())(lambda: self.taken(n_x, k, 5).wait_recv())
        self.taken(5 * n_x - 1, k, 4).wait_recv()
        first = jnp.where(z <= 3, 3 - z, jnp.where(z <= 5, 0, 11 - z))
        total = jnp.zeros((self.share, HEAD), F32)
        for i in range(n_x * ENTRIES):
            j = n_x * ENTRIES - 1 - i if self.reverse else i
            spot = self.spot(k, j // ENTRIES, lax.rem(first + j % ENTRIES, ENTRIES))
            self.outbox[spot, :] = total.astype(BF16)
            total = total + self.inbox[spot, :].astype(F32)

        def give_group(x, side):
            self.copy(
                self.outbox.at[self.spot(k, x, 1 + 4 * side)],
                self.back.at[self.tile_part(k, side, 3, self.x)],
                k,
                6,
                8 + side,
                x,
                self.ring(4 * side - 2),
            ).start()

        for i in range(n_x):
            x = lax.rem(self.x + (i + 1), n_x)
            give_group(x, 0)
            give_group(x, 1)

        @pl.when(self.odd_owner())
        def _():
            for i in range(n_x):
                x = lax.rem(self.x + (i + 1), n_x)
                target = self.back.at[self.tile_part(k, 2, 3, self.x)]
                to = jnp.where(z == 2, RING - 1, 0)
                self.copy(self.outbox.at[self.spot(k, x, 0)], target, k, 7, 7, x, to).start()

    def give_near(self, k):
        z, n_x = self.z, self.n_x

        def give(x, to, entry, kind):
            self.copy(
                self.outbox.at[self.spot(k, x, entry)], self.result.at[self.piece(z, k, self.x)], k, kind, kind, x, to
            ).start()

        for i in range(n_x):
            x = lax.rem(self.x + (i + 1), n_x)
            give(x, self.ring(-1), 2, 6)
            give(x, self.ring(1), 4, 6)
            if i < n_x - 1:
                give(x, z, 3, 6)
        self.result[self.piece(z, k, self.x), :] = self.outbox[self.spot(k, self.x, 3), :]

    def pass_on(self, k):
        z = self.z
        for side in range(2):
            c = self.ring(2 - 4 * side)
            self.taken(self.n_x, k, 8 + side).wait_recv()
            base = self.back[self.tile(k, side, 3), :].astype(F32)
            mine = self.state[self.head(c, k), :].astype(F32)
            near = self.child[self.tile(k, 2 * side, 5), :].astype(F32)
            far = self.child[self.tile(k, 2 * side + 1, 5), :].astype(F32)
            if (side == 0) != self.reverse:
                for_far = base
                for_near = base + far
                for_mine = for_near + near
            else:
                for_mine = base
                for_near = base + mine
                for_far = for_near + near
            self.down[self.tile(k, 2 * side + 1, 5), :] = for_far.astype(BF16)
            self.down[self.tile(k, 2 * side, 5), :] = for_near.astype(BF16)
            self.result[self.head(c, k), :] = for_mine.astype(BF16)

        def hand(side, slot, to, send, recv):
            self.copy(
                self.down.at[self.tile(k, slot, 5)],
                self.result.at[self.head(self.ring(2 - 4 * side), k)],
                k,
                send,
                recv,
                self.x,
                to,
            ).start()

        pl.when(self.even_inner())(lambda: hand(0, 1, z - 2, 10, 12))
        pl.when(self.odd_inner())(lambda: hand(1, 3, z + 2, 10, 12))
        pl.when(z != 0)(lambda: hand(0, 0, z - 1, 8, 10))
        pl.when(z != RING - 1)(lambda: hand(1, 2, z + 1, 9, 11))

        @pl.when(self.odd())
        def _():
            self.taken(self.n_x, k, 7).wait_recv()
            c = self.odd_target()
            base = self.back[self.tile(k, 2, 3), :].astype(F32)
            mine = base + self.child[self.tile(k, 4, 5), :].astype(F32)
            theirs = base + self.state[self.head(c, k), :].astype(F32)
            their_turn = (z == RING - 1) != self.reverse
            self.down[self.tile(k, 4, 5), :] = jnp.where(their_turn, base, theirs).astype(BF16)
            self.result[self.head(c, k), :] = jnp.where(their_turn, mine, base).astype(BF16)
            to = jnp.where(z == 0, 1, RING - 2)
            self.copy(
                self.down.at[self.tile(k, 4, 5)], self.result.at[self.head(c, k)], k, 10, 12, self.x, to
            ).start()

    def arrive(self, k):
        z, n_x = self.z, self.n_x
        self.taken(3 * n_x - 1, k, 6).wait_recv()
        pl.when(z != RING - 1)(lambda: self.taken(n_x, k, 10).wait_recv())
        pl.when(z != 0)(lambda: self.taken(n_x, k, 11).wait_recv())
        self.taken(n_x, k, 12).wait_recv()

    def drain(self, k):
        z, n_x = self.z, self.n_x

        def sent(count, kind):
            self.taken(count, k, kind).wait_send()

        pl.when(z != RING - 1)(lambda: sent(n_x, 0))
        pl.when(z != 0)(lambda: sent(n_x, 1))
        sent(n_x, 2)
        sent(5 * n_x - 1, 4)
        pl.when(self.odd())(lambda: sent(n_x, 5))
        sent(5 * n_x - 1, 6)
        pl.when(self.odd_owner())(lambda: sent(n_x, 7))
        pl.when(z != 0)(lambda: sent(n_x, 8))
        pl.when(z != RING - 1)(lambda: sent(n_x, 9))
        sent(n_x, 10)


PASS_REFS = 8
KINDS = 14


def pass_scratch(n_x):
    tiles = CHUNKS * HEAD
    sizes = (
        HEADS * HEAD,
        5 * tiles,
        3 * tiles,
        ENTRIES * tiles,
        ENTRIES * tiles,
        3 * tiles,
        5 * tiles,
        HEADS * HEAD,
    )
    return [pltpu.VMEM((size, HEAD), BF16) for size in sizes]


def chunk_loop(k, body):
    @pl.loop(0, HEADS // CHUNKS // 4)
    def _(step):
        for inner in range(4):
            body((step * 4 + inner) * CHUNKS + k)


def kernel(
    n_seq,
    n_dp,
    q_hbm,
    k_hbm,
    v_hbm,
    gain_hbm,
    cot_hbm,
    out_hbm,
    gq_hbm,
    gk_hbm,
    gv_hbm,
    gg_hbm,
    q_ref,
    k_ref,
    v_ref,
    cot_ref,
    gain_ref,
    att_ref,
    score_ref,
    ga_ref,
    gk_part,
    gv_part,
    out_ref,
    gq_ref,
    gk_ref,
    gv_ref,
    *rest,
):
    ahead_refs, rest = rest[:PASS_REFS], rest[PASS_REFS:]
    behind_refs, rest = rest[:PASS_REFS], rest[PASS_REFS:]
    gain_part, gain_r1, gain_s2, gain_r2, gain_r3, gain_out, *sems = rest
    load_sem, store_sem, send_sem, recv_sem, gain_send_sem, gain_recv_sem = sems
    seq = lax.axis_index("seq")
    dp = lax.axis_index("dp")
    n_x = n_seq // RING
    ahead = ScanPass(0, False, ahead_refs, send_sem, recv_sem, n_x)
    behind = ScanPass(1, True, behind_refs, send_sem, recv_sem, n_x)
    tokens = q_ref.shape[0]
    features = HEADS * HEAD
    scaling = HEAD ** (-0.5)
    grows = HEADS // n_dp

    def cols(h):
        return pl.ds(pl.multiple_of(h * HEAD, HEAD), HEAD)

    loads = [
        pltpu.make_async_copy(k_hbm.at[0], k_ref, load_sem.at[0]),
        pltpu.make_async_copy(v_hbm.at[0], v_ref, load_sem.at[1]),
        pltpu.make_async_copy(q_hbm.at[0], q_ref, load_sem.at[2]),
        pltpu.make_async_copy(cot_hbm.at[0], cot_ref, load_sem.at[3]),
        pltpu.make_async_copy(gain_hbm, gain_ref, load_sem.at[4]),
    ]
    for load in loads:
        load.start()

    barrier = pltpu.get_barrier_semaphore()

    @pl.loop(1, n_seq)
    def _(k):
        peer = lax.rem(seq + k, n_seq)
        pl.semaphore_signal(barrier, inc=1, device_id={"seq": peer}, device_id_type=MESH)

    @pl.loop(1, n_dp)
    def _(k):
        peer = lax.rem(dp + k, n_dp)
        pl.semaphore_signal(barrier, inc=1, device_id={"dp": peer}, device_id_type=MESH)

    ahead.clear()
    behind.clear()

    position_t = lax.broadcasted_iota(jnp.int32, (tokens, tokens), 0)
    position_u = lax.broadcasted_iota(jnp.int32, (tokens, tokens), 1)
    causal = position_t >= position_u

    loads[0].wait()
    loads[1].wait()

    def state_of(h):
        c = cols(h)
        ahead.state[c, :] = dot(k_ref[:, c], v_ref[:, c], 0, 0).astype(BF16)

    chunk_loop(0, state_of)
    pl.semaphore_wait(barrier, n_seq - 1 + n_dp - 1)
    ahead.send_far(0)
    chunk_loop(1, state_of)
    ahead.send_far(1)
    ahead.send_near(0)
    ahead.send_near(1)

    loads[2].wait()
    loads[3].wait()
    loads[4].wait()

    def local_of(h):
        c = cols(h)
        raw = dot(q_ref[:, c], k_ref[:, c], 1, 1)
        score = jnp.where(causal, raw * scaling, 0.0).astype(BF16)
        score_ref[c, :] = score
        att_ref[:, c] = dot(score, v_ref[:, c], 1, 0)

    chunk_loop(0, local_of)
    ahead.relay(0)
    ahead.relay(1)
    chunk_loop(1, local_of)
    ahead.own(0)
    ahead.own(1)
    ahead.give_near(0)
    ahead.give_near(1)
    ahead.pass_on(0)
    ahead.pass_on(1)

    def attend(chunk, step, carry):
        squares, inner = carry
        for k in range(4):
            h = (step * 4 + k) * CHUNKS + chunk
            c = cols(h)
            att = att_ref[:, c] + scaling * dot(q_ref[:, c], ahead.result[c, :], 1, 0)
            att_ref[:, c] = att
            squares = squares + att * att
            inner = inner + att * (cot_ref[:, c].astype(F32) * gain_ref[pl.ds(h, 1), :])
        return squares, inner

    zero = jnp.zeros((tokens, HEAD), F32)
    carry = (zero, zero)
    for chunk in range(CHUNKS):
        ahead.arrive(chunk)
        carry = lax.fori_loop(0, HEADS // CHUNKS // 4, functools.partial(attend, chunk), carry)
    squares, inner = carry
    root = jnp.sqrt(jnp.sum(squares, axis=1, keepdims=True) / features + EPSILON)
    inverse = 1.0 / root
    mean = jnp.sum(inner, axis=1, keepdims=True) * inverse / features

    def normalize(h):
        c = cols(h)
        weight = gain_ref[pl.ds(h, 1), :]
        upstream = cot_ref[:, c].astype(F32)
        normalized = att_ref[:, c] * inverse
        out_ref[:, c] = (weight * normalized).astype(BF16)
        gain_part[h] = jnp.sum(upstream * normalized, axis=0, keepdims=True)
        grad = ((upstream * weight - normalized * mean) * inverse).astype(BF16)
        ga_ref[:, c] = grad
        behind.state[c, :] = (scaling * dot(q_ref[:, c], grad, 0, 0)).astype(BF16)

    chunk_loop(0, normalize)
    behind.send_far(0)
    chunk_loop(1, normalize)
    behind.send_far(1)
    behind.send_near(0)
    behind.send_near(1)

    def gain_copy(src, dst, index, axis, peer):
        return pltpu.make_async_remote_copy(
            src_ref=src,
            dst_ref=dst,
            send_sem=gain_send_sem.at[index],
            recv_sem=gain_recv_sem.at[index],
            device_id={axis: peer},
            device_id_type=MESH,
        )

    def part(j):
        return pl.ds(j * grows, grows)

    @pl.loop(1, n_dp)
    def _(k):
        peer = lax.rem(dp + k, n_dp)
        gain_copy(gain_part.at[part(peer)], gain_r1.at[part(dp)], 0, "dp", peer).start()

    store_out = pltpu.make_async_copy(out_ref, out_hbm.at[0], store_sem.at[0])
    store_out.start()

    def grads(h):
        c = cols(h)
        grad = ga_ref[:, c]
        gs = jnp.where(causal, dot(grad, v_ref[:, c], 1, 1), 0.0).astype(BF16)
        query = dot(gs, k_ref[:, c], 1, 0) + dot(grad, ahead.result[c, :], 1, 1)
        gq_ref[:, c] = (scaling * query).astype(BF16)
        gk_part[:, c] = scaling * dot(gs, q_ref[:, c], 0, 0)
        gv_part[:, c] = dot(score_ref[c, :], grad, 0, 0)

    chunk_loop(0, grads)
    behind.relay(0)
    behind.relay(1)
    chunk_loop(1, grads)
    store_gq = pltpu.make_async_copy(gq_ref, gq_hbm.at[0], store_sem.at[1])
    store_gq.start()

    gain_r1[part(dp)] = gain_part[part(dp)]
    others = pl.ds(0, (n_dp - 1) * grows)
    first = gain_copy(gain_part.at[others], gain_r1.at[others], 0, "dp", lax.rem(dp + 1, n_dp))
    first.wait_recv()
    summed = jnp.zeros((grows, 1, HEAD), F32)
    for j in range(n_dp):
        summed = summed + gain_r1[pl.ds(j * grows, grows)]
    gain_s2[...] = summed

    @pl.loop(1, n_seq)
    def _(k):
        peer = lax.rem(seq + k, n_seq)
        gain_copy(gain_s2, gain_r2.at[pl.ds(seq * grows, grows)], 1, "seq", peer).start()

    behind.own(0)
    behind.own(1)
    behind.give_near(0)
    behind.give_near(1)

    behind.pass_on(0)
    behind.pass_on(1)

    gain_r2[pl.ds(seq * grows, grows)] = summed
    some = pl.ds(0, (n_seq - 1) * grows)
    second = gain_copy(gain_r2.at[some], gain_r2.at[some], 1, "seq", lax.rem(seq + 1, n_seq))
    second.wait_recv()

    def add(j, total):
        return total + gain_r2[pl.ds(j * grows, grows)]

    total = lax.fori_loop(0, n_seq, add, jnp.zeros((grows, 1, HEAD), F32)) / n_dp
    gain_r3[part(dp)] = total

    @pl.loop(1, n_dp)
    def _(k):
        peer = lax.rem(dp + k, n_dp)
        gain_copy(gain_r3.at[part(dp)], gain_r3.at[part(dp)], 2, "dp", peer).start()


    def finish(h):
        c = cols(h)
        suffix = behind.result[c, :]
        gk_ref[:, c] = (gk_part[:, c] + dot(v_ref[:, c], suffix, 1, 1)).astype(BF16)
        gv_ref[:, c] = (gv_part[:, c] + dot(k_ref[:, c], suffix, 1, 0)).astype(BF16)

    for chunk in range(CHUNKS):
        behind.arrive(chunk)
        chunk_loop(chunk, finish)
    store_gk = pltpu.make_async_copy(gk_ref, gk_hbm.at[0], store_sem.at[2])
    store_gv = pltpu.make_async_copy(gv_ref, gv_hbm.at[0], store_sem.at[3])
    store_gk.start()
    store_gv.start()

    third = gain_copy(gain_r3.at[others], gain_r3.at[others], 2, "dp", lax.rem(dp + 1, n_dp))
    third.wait_recv()
    for h in range(HEADS):
        gain_out[h : h + 1, :] = gain_r3[h]
    store_gain = pltpu.make_async_copy(gain_out, gg_hbm, store_sem.at[4])
    store_gain.start()

    for chunk in range(CHUNKS):
        ahead.drain(chunk)
        behind.drain(chunk)
    first.wait_send()
    second.wait_send()
    third.wait_send()
    for store in (store_out, store_gq, store_gk, store_gv, store_gain):
        store.wait()


def hand_out(*refs):
    sources, targets, sem = refs[:5], refs[5:10], refs[10]
    stores = [pltpu.make_async_copy(a, b, sem.at[i]) for i, (a, b) in enumerate(zip(sources, targets))]
    for store in stores:
        store.start()
    for store in stores:
        store.wait()


def stay(array):
    return pltpu.with_memory_space_constraint(array, pltpu.HBM)


def solution(mesh):
    n_seq = mesh.shape["seq"]
    n_dp = mesh.shape["dp"]

    def per_device(queries, keys, values, gain, cotangent):
        _, tokens, features = queries.shape
        grows = HEADS // n_dp
        exact = pltpu.VMEM((tokens, features), F32)
        half = pltpu.VMEM((tokens, features), BF16)
        big = jax.ShapeDtypeStruct(queries.shape, BF16)
        anywhere = pl.BlockSpec(memory_space=pl.ANY)
        results = pl.pallas_call(
            functools.partial(kernel, n_seq, n_dp),
            out_shape=(big, big, big, big, jax.ShapeDtypeStruct((HEADS, HEAD), F32)),
            in_specs=[pl.BlockSpec(memory_space=pltpu.HBM)] * 5,
            out_specs=(anywhere,) * 5,
            scratch_shapes=[
                half,
                half,
                half,
                half,
                pltpu.VMEM((HEADS, HEAD), F32),
                exact,
                pltpu.VMEM((features, tokens), BF16),
                half,
                exact,
                exact,
                half,
                half,
                half,
                half,
            ]
            + pass_scratch(n_seq // RING) * 2
            + [
                pltpu.VMEM((HEADS, 1, HEAD), F32),
                pltpu.VMEM((HEADS, 1, HEAD), F32),
                pltpu.VMEM((grows, 1, HEAD), F32),
                pltpu.VMEM((n_seq * grows, 1, HEAD), F32),
                pltpu.VMEM((HEADS, 1, HEAD), F32),
                pltpu.VMEM((HEADS, HEAD), F32),
                pltpu.SemaphoreType.DMA((5,)),
                pltpu.SemaphoreType.DMA((5,)),
                pltpu.SemaphoreType.DMA((2, CHUNKS, KINDS)),
                pltpu.SemaphoreType.DMA((2, CHUNKS, KINDS)),
                pltpu.SemaphoreType.DMA((3,)),
                pltpu.SemaphoreType.DMA((3,)),
            ],
            compiler_params=pltpu.CompilerParams(
                collective_id=0, has_side_effects=True, vmem_limit_bytes=32 * 2**20
            ),
        )(*(stay(a) for a in (queries, keys, values, gain.reshape(HEADS, HEAD), cotangent)))
        small = jax.ShapeDtypeStruct((HEADS, HEAD), F32)
        results = pl.pallas_call(
            hand_out,
            out_shape=(big, big, big, big, small),
            in_specs=[anywhere] * 5,
            out_specs=(anywhere,) * 5,
            scratch_shapes=[pltpu.SemaphoreType.DMA((5,))],
            compiler_params=pltpu.CompilerParams(vmem_limit_bytes=2**20),
        )(*results)
        return (*results[:4], results[4].reshape(features))

    sharded = P("dp", "seq", None)
    return jax.shard_map(
        per_device,
        mesh=mesh,
        in_specs=(sharded, sharded, sharded, P(), sharded),
        out_specs=(sharded, sharded, sharded, sharded, P()),
        check_vma=False,
    )
```

```python
import functools

import jax
import jax.numpy as jnp
from jax import lax
from jax.experimental import pallas as pl
from jax.experimental.pallas import tpu as pltpu
from jax.sharding import PartitionSpec as P

HEADS = 16
HEAD = 128
EPSILON = 1e-06
RING = 8
CHUNKS = 2
ENTRIES = 6
MESH = pl.DeviceIdType.MESH
F32 = jnp.float32
BF16 = jnp.bfloat16


def dot(a, b, ca, cb):
    return lax.dot_general(a, b, (((ca,), (cb,)), ((), ())), preferred_element_type=F32)


class ScanPass:
    def __init__(self, index, reverse, refs, send_sem, recv_sem, n_x):
        self.state, self.child, self.group, self.inbox, self.outbox, self.back, self.down, self.result = refs
        self.index, self.reverse, self.n_x = index, reverse, n_x
        self.send_sem, self.recv_sem = send_sem, recv_sem
        seq = lax.axis_index("seq")
        self.x, self.z = seq // RING, lax.rem(seq, RING)
        self.share = HEAD // n_x

    def ring(self, offset):
        return lax.rem(self.z + (offset + RING), RING)

    def rows(self, start, size):
        return pl.ds(pl.multiple_of(start, self.share), size)

    def head(self, c, k):
        return self.rows((k * RING + c) * HEAD, HEAD)

    def piece(self, c, k, x):
        return self.rows((k * RING + c) * HEAD + x * self.share, self.share)

    def spot(self, k, x, entry):
        return self.rows(((k * self.n_x + x) * ENTRIES + entry) * self.share, self.share)

    def tile(self, k, i, count):
        return self.rows((k * count + i) * HEAD, HEAD)

    def tile_part(self, k, i, count, x):
        return self.rows((k * count + i) * HEAD + x * self.share, self.share)

    def copy(self, src, dst, k, send, recv, x, z):
        return pltpu.make_async_remote_copy(
            src_ref=src,
            dst_ref=dst,
            send_sem=self.send_sem.at[self.index, k, send],
            recv_sem=self.recv_sem.at[self.index, k, recv],
            device_id={"seq": x * RING + z},
            device_id_type=MESH,
        )

    def taken(self, count, k, kind):
        part = pl.ds(0, count * self.share)
        return self.copy(self.state.at[part], self.result.at[part], k, kind, kind, self.x, self.ring(1))

    def odd(self):
        return jnp.logical_or(self.z == 0, self.z == RING - 1)

    def even_inner(self):
        return jnp.logical_and(self.z != 0, lax.rem(self.z, 2) == 0)

    def odd_inner(self):
        return jnp.logical_and(self.z != RING - 1, lax.rem(self.z, 2) == 1)

    def odd_owner(self):
        return jnp.logical_or(self.z == 2, self.z == 5)

    def odd_target(self):
        return jnp.where(self.z == 0, 5, 2)

    def clear(self):
        zero = jnp.zeros((HEAD, HEAD), BF16)
        few = jnp.zeros((self.share, HEAD), BF16)

        def blank(slot):
            for k in range(CHUNKS):
                self.child[self.tile(k, slot, 5), :] = zero

        pl.when(self.z == 0)(lambda: blank(0))
        pl.when(self.z == RING - 1)(lambda: blank(2))
        pl.when(jnp.logical_not(self.even_inner()))(lambda: blank(1))
        pl.when(jnp.logical_not(self.odd_inner()))(lambda: blank(3))

        @pl.when(jnp.logical_not(self.odd_owner()))
        def _():
            for k in range(CHUNKS):
                for x in range(self.n_x):
                    self.inbox[self.spot(k, x, 0), :] = few

    def send_far(self, k):
        z = self.z

        def hand(offset, to, slot, send):
            self.copy(
                self.state.at[self.head(self.ring(offset), k)],
                self.child.at[self.tile(k, slot, 5)],
                k,
                send,
                slot if slot < 4 else 13,
                self.x,
                to,
            ).start()

        even = lax.rem(z, 2) == 0
        pl.when(jnp.logical_and(even, z != 6))(lambda: hand(4, z + 2, 1, 2))
        pl.when(jnp.logical_not(jnp.logical_or(even, z == 1)))(lambda: hand(4, z - 2, 3, 2))
        pl.when(z == 6)(lambda: hand(4, z + 1, 4, 2))
        pl.when(z == 1)(lambda: hand(4, z - 1, 4, 2))
        pl.when(z != RING - 1)(lambda: hand(3, z + 1, 0, 0))
        pl.when(z != 0)(lambda: hand(-3, z - 1, 2, 1))

    def send_near(self, k):
        z, n_x = self.z, self.n_x

        def direct(c, x, entry, kind):
            self.copy(
                self.state.at[self.piece(c, k, x)], self.inbox.at[self.spot(k, self.x, entry)], k, kind, kind, x, c
            ).start()

        for i in range(n_x):
            x = lax.rem(self.x + (i + 1), n_x)
            direct(self.ring(1), x, 2, 4)
            direct(self.ring(-1), x, 4, 4)
            if i < n_x - 1:
                direct(z, x, 3, 4)
        self.inbox[self.spot(k, self.x, 3), :] = self.state[self.piece(z, k, self.x), :]

    def relay(self, k):
        z, n_x = self.z, self.n_x
        whole = n_x
        for side in range(2):
            if side == 0:
                pl.when(z != 0)(lambda: self.taken(whole, k, 0).wait_recv())
                pl.when(self.even_inner())(lambda: self.taken(whole, k, 1).wait_recv())
            else:
                pl.when(z != RING - 1)(lambda: self.taken(whole, k, 2).wait_recv())
                pl.when(self.odd_inner())(lambda: self.taken(whole, k, 3).wait_recv())
            c = self.ring(2 - 4 * side)
            total = self.state[self.head(c, k), :].astype(F32)
            total = total + self.child[self.tile(k, 2 * side, 5), :].astype(F32)
            total = total + self.child[self.tile(k, 2 * side + 1, 5), :].astype(F32)
            self.group[self.tile(k, side, 3), :] = total.astype(BF16)
            for i in range(n_x):
                x = lax.rem(self.x + (i + 1), n_x)
                self.copy(
                    self.group.at[self.tile_part(k, side, 3, x)],
                    self.inbox.at[self.spot(k, self.x, 1 + 4 * side)],
                    k,
                    4,
                    4,
                    x,
                    c,
                ).start()

        @pl.when(self.odd())
        def _():
            self.taken(whole, k, 13).wait_recv()
            c = self.odd_target()
            total = self.state[self.head(c, k), :].astype(F32) + self.child[self.tile(k, 4, 5), :].astype(F32)
            self.group[self.tile(k, 2, 3), :] = total.astype(BF16)
            for i in range(n_x):
                x = lax.rem(self.x + (i + 1), n_x)
                source = self.group.at[self.tile_part(k, 2, 3, x)]
                self.copy(source, self.inbox.at[self.spot(k, self.x, 0)], k, 5, 5, x, c).start()

    def own(self, k):
        z, n_x = self.z, self.n_x
        pl.when(self.odd_owner())(lambda: self.taken(n_x, k, 5).wait_recv())
        self.taken(5 * n_x - 1, k, 4).wait_recv()
        first = jnp.where(z <= 3, 3 - z, jnp.where(z <= 5, 0, 11 - z))
        total = jnp.zeros((self.share, HEAD), F32)
        for i in range(n_x * ENTRIES):
            j = n_x * ENTRIES - 1 - i if self.reverse else i
            spot = self.spot(k, j // ENTRIES, lax.rem(first + j % ENTRIES, ENTRIES))
            self.outbox[spot, :] = total.astype(BF16)
            total = total + self.inbox[spot, :].astype(F32)

        def give_group(x, side):
            self.copy(
                self.outbox.at[self.spot(k, x, 1 + 4 * side)],
                self.back.at[self.tile_part(k, side, 3, self.x)],
                k,
                6,
                8 + side,
                x,
                self.ring(4 * side - 2),
            ).start()

        for i in range(n_x):
            x = lax.rem(self.x + (i + 1), n_x)
            give_group(x, 0)
            give_group(x, 1)

        @pl.when(self.odd_owner())
        def _():
            for i in range(n_x):
                x = lax.rem(self.x + (i + 1), n_x)
                target = self.back.at[self.tile_part(k, 2, 3, self.x)]
                to = jnp.where(z == 2, RING - 1, 0)
                self.copy(self.outbox.at[self.spot(k, x, 0)], target, k, 7, 7, x, to).start()

    def give_near(self, k):
        z, n_x = self.z, self.n_x

        def give(x, to, entry, kind):
            self.copy(
                self.outbox.at[self.spot(k, x, entry)], self.result.at[self.piece(z, k, self.x)], k, kind, kind, x, to
            ).start()

        for i in range(n_x):
            x = lax.rem(self.x + (i + 1), n_x)
            give(x, self.ring(-1), 2, 6)
            give(x, self.ring(1), 4, 6)
            if i < n_x - 1:
                give(x, z, 3, 6)
        self.result[self.piece(z, k, self.x), :] = self.outbox[self.spot(k, self.x, 3), :]

    def pass_on(self, k):
        z = self.z
        for side in range(2):
            c = self.ring(2 - 4 * side)
            self.taken(self.n_x, k, 8 + side).wait_recv()
            base = self.back[self.tile(k, side, 3), :].astype(F32)
            mine = self.state[self.head(c, k), :].astype(F32)
            near = self.child[self.tile(k, 2 * side, 5), :].astype(F32)
            far = self.child[self.tile(k, 2 * side + 1, 5), :].astype(F32)
            if (side == 0) != self.reverse:
                for_far = base
                for_near = base + far
                for_mine = for_near + near
            else:
                for_mine = base
                for_near = base + mine
                for_far = for_near + near
            self.down[self.tile(k, 2 * side + 1, 5), :] = for_far.astype(BF16)
            self.down[self.tile(k, 2 * side, 5), :] = for_near.astype(BF16)
            self.result[self.head(c, k), :] = for_mine.astype(BF16)

        def hand(side, slot, to, send, recv):
            self.copy(
                self.down.at[self.tile(k, slot, 5)],
                self.result.at[self.head(self.ring(2 - 4 * side), k)],
                k,
                send,
                recv,
                self.x,
                to,
            ).start()

        pl.when(self.even_inner())(lambda: hand(0, 1, z - 2, 10, 12))
        pl.when(self.odd_inner())(lambda: hand(1, 3, z + 2, 10, 12))
        pl.when(z != 0)(lambda: hand(0, 0, z - 1, 8, 10))
        pl.when(z != RING - 1)(lambda: hand(1, 2, z + 1, 9, 11))

        @pl.when(self.odd())
        def _():
            self.taken(self.n_x, k, 7).wait_recv()
            c = self.odd_target()
            base = self.back[self.tile(k, 2, 3), :].astype(F32)
            mine = base + self.child[self.tile(k, 4, 5), :].astype(F32)
            theirs = base + self.state[self.head(c, k), :].astype(F32)
            their_turn = (z == RING - 1) != self.reverse
            self.down[self.tile(k, 4, 5), :] = jnp.where(their_turn, base, theirs).astype(BF16)
            self.result[self.head(c, k), :] = jnp.where(their_turn, mine, base).astype(BF16)
            to = jnp.where(z == 0, 1, RING - 2)
            self.copy(
                self.down.at[self.tile(k, 4, 5)], self.result.at[self.head(c, k)], k, 10, 12, self.x, to
            ).start()

    def arrive(self, k):
        z, n_x = self.z, self.n_x
        self.taken(3 * n_x - 1, k, 6).wait_recv()
        pl.when(z != RING - 1)(lambda: self.taken(n_x, k, 10).wait_recv())
        pl.when(z != 0)(lambda: self.taken(n_x, k, 11).wait_recv())
        self.taken(n_x, k, 12).wait_recv()

    def drain(self, k):
        z, n_x = self.z, self.n_x

        def sent(count, kind):
            self.taken(count, k, kind).wait_send()

        pl.when(z != RING - 1)(lambda: sent(n_x, 0))
        pl.when(z != 0)(lambda: sent(n_x, 1))
        sent(n_x, 2)
        sent(5 * n_x - 1, 4)
        pl.when(self.odd())(lambda: sent(n_x, 5))
        sent(5 * n_x - 1, 6)
        pl.when(self.odd_owner())(lambda: sent(n_x, 7))
        pl.when(z != 0)(lambda: sent(n_x, 8))
        pl.when(z != RING - 1)(lambda: sent(n_x, 9))
        sent(n_x, 10)


PASS_REFS = 8
KINDS = 14


def pass_scratch(n_x):
    tiles = CHUNKS * HEAD
    sizes = (
        HEADS * HEAD,
        5 * tiles,
        3 * tiles,
        ENTRIES * tiles,
        ENTRIES * tiles,
        3 * tiles,
        5 * tiles,
        HEADS * HEAD,
    )
    return [pltpu.VMEM((size, HEAD), BF16) for size in sizes]


def chunk_loop(k, body):
    @pl.loop(0, RING // 4)
    def _(step):
        for inner in range(4):
            body(k * RING + step * 4 + inner)


def kernel(
    n_seq,
    n_dp,
    q_hbm,
    k_hbm,
    v_hbm,
    gain_hbm,
    cot_hbm,
    out_hbm,
    gq_hbm,
    gk_hbm,
    gv_hbm,
    gg_hbm,
    q_ref,
    k_ref,
    v_ref,
    cot_ref,
    gain_ref,
    att_ref,
    score_ref,
    ga_ref,
    gk_part,
    gv_part,
    out_ref,
    gq_ref,
    gk_ref,
    gv_ref,
    *rest,
):
    ahead_refs, rest = rest[:PASS_REFS], rest[PASS_REFS:]
    behind_refs, rest = rest[:PASS_REFS], rest[PASS_REFS:]
    gain_part, gain_r1, gain_s2, gain_r2, gain_s3, gain_r3, gain_r4, gain_out, *sems = rest
    load_sem, store_sem, send_sem, recv_sem, gain_send_sem, gain_recv_sem = sems
    seq = lax.axis_index("seq")
    dp = lax.axis_index("dp")
    n_x = n_seq // RING
    ahead = ScanPass(0, False, ahead_refs, send_sem, recv_sem, n_x)
    behind = ScanPass(1, True, behind_refs, send_sem, recv_sem, n_x)
    tokens = q_ref.shape[0]
    features = HEADS * HEAD
    scaling = HEAD ** (-0.5)
    grows = HEADS // n_x

    def cols(h):
        return pl.ds(pl.multiple_of(h * HEAD, HEAD), HEAD)

    half = features // CHUNKS
    early = []
    for k in range(CHUNKS):
        for i, (src, dst) in enumerate(((k_hbm, k_ref), (v_hbm, v_ref))):
            part_of = pl.ds(k * half, half)
            early.append(
                pltpu.make_async_copy(src.at[0, :, part_of], dst.at[:, part_of], load_sem.at[CHUNKS * k + i])
            )
    loads = [
        pltpu.make_async_copy(q_hbm.at[0], q_ref, load_sem.at[4]),
        pltpu.make_async_copy(cot_hbm.at[0], cot_ref, load_sem.at[5]),
        pltpu.make_async_copy(gain_hbm, gain_ref, load_sem.at[6]),
    ]
    for load in early + loads:
        load.start()

    barrier = pltpu.get_barrier_semaphore()

    for step in range(n_x):
        for offset in (1, -1, 2, -2, 0, 3, -3, 4):
            if step == 0 and offset == 0:
                continue
            peer = lax.rem(ahead.x + step, n_x) * RING + ahead.ring(offset)
            pl.semaphore_signal(barrier, inc=1, device_id={"seq": peer}, device_id_type=MESH)

    @pl.loop(1, n_dp)
    def _(k):
        peer = lax.rem(dp + k, n_dp)
        pl.semaphore_signal(barrier, inc=1, device_id={"dp": peer}, device_id_type=MESH)

    ahead.clear()
    behind.clear()

    position_t = lax.broadcasted_iota(jnp.int32, (tokens, tokens), 0)
    position_u = lax.broadcasted_iota(jnp.int32, (tokens, tokens), 1)
    causal = position_t >= position_u

    def state_of(h):
        c = cols(h)
        ahead.state[c, :] = dot(k_ref[:, c], v_ref[:, c], 0, 0).astype(BF16)

    early[0].wait()
    early[1].wait()
    chunk_loop(0, state_of)
    pl.semaphore_wait(barrier, n_seq - 1 + n_dp - 1)
    ahead.send_far(0)
    early[2].wait()
    early[3].wait()
    chunk_loop(1, state_of)
    ahead.send_far(1)
    ahead.send_near(0)
    ahead.send_near(1)

    for load in loads:
        load.wait()

    def local_of(h):
        c = cols(h)
        raw = dot(q_ref[:, c], k_ref[:, c], 1, 1)
        score = jnp.where(causal, raw * scaling, 0.0).astype(BF16)
        score_ref[c, :] = score
        att_ref[:, c] = dot(score, v_ref[:, c], 1, 0)

    chunk_loop(0, local_of)
    ahead.relay(0)
    ahead.relay(1)
    chunk_loop(1, local_of)
    ahead.own(0)
    ahead.own(1)
    ahead.give_near(0)
    ahead.give_near(1)
    ahead.pass_on(0)
    ahead.pass_on(1)

    def attend(chunk, step, carry):
        squares, inner = carry
        for k in range(4):
            h = chunk * RING + step * 4 + k
            c = cols(h)
            att = att_ref[:, c] + scaling * dot(q_ref[:, c], ahead.result[c, :], 1, 0)
            att_ref[:, c] = att
            squares = squares + att * att
            inner = inner + att * (cot_ref[:, c].astype(F32) * gain_ref[pl.ds(h, 1), :])
        return squares, inner

    zero = jnp.zeros((tokens, HEAD), F32)
    carry = (zero, zero)
    for chunk in range(CHUNKS):
        ahead.arrive(chunk)
        carry = lax.fori_loop(0, RING // 4, functools.partial(attend, chunk), carry)
    squares, inner = carry
    root = jnp.sqrt(jnp.sum(squares, axis=1, keepdims=True) / features + EPSILON)
    inverse = 1.0 / root
    mean = jnp.sum(inner, axis=1, keepdims=True) * inverse / features

    def pull(h):
        c = cols(h)
        upstream = cot_ref[:, c].astype(F32)
        normalized = att_ref[:, c] * inverse
        grad = ((upstream * gain_ref[pl.ds(h, 1), :] - normalized * mean) * inverse).astype(BF16)
        ga_ref[:, c] = grad
        behind.state[c, :] = (scaling * dot(q_ref[:, c], grad, 0, 0)).astype(BF16)

    def normalize(h):
        c = cols(h)
        normalized = att_ref[:, c] * inverse
        out_ref[:, c] = (gain_ref[pl.ds(h, 1), :] * normalized).astype(BF16)

    def gain_of(h):
        c = cols(h)
        gain_part[h] = jnp.sum(cot_ref[:, c].astype(F32) * (att_ref[:, c] * inverse), axis=0, keepdims=True)

    x, z = seq // RING, lax.rem(seq, RING)

    def gain_copy(src, dst, index, axis, peer):
        return pltpu.make_async_remote_copy(
            src_ref=src,
            dst_ref=dst,
            send_sem=gain_send_sem.at[index],
            recv_sem=gain_recv_sem.at[index],
            device_id={axis: peer},
            device_id_type=MESH,
        )

    def part(j):
        return pl.ds(j * grows, grows)

    def added(parts, count):
        total = parts[part(0)]
        for j in range(1, count):
            total = total + parts[part(j)]
        return total

    def gain_round(src_of, dst, index, axis, me, count, peer_of):
        @pl.loop(1, count)
        def _(k):
            at = lax.rem(me + k, count)
            gain_copy(src_of(at), dst.at[part(me)], index, axis, peer_of(at)).start()

        rest = pl.ds(0, (count - 1) * grows)
        return gain_copy(dst.at[rest], dst.at[rest], index, axis, peer_of(lax.rem(me + 1, count)))

    def on_x(at):
        return at * RING + z

    chunk_loop(0, pull)
    behind.send_far(0)
    chunk_loop(1, pull)
    behind.send_far(1)
    chunk_loop(0, gain_of)
    chunk_loop(1, gain_of)
    behind.send_near(0)
    behind.send_near(1)
    first = gain_round(lambda at: gain_part.at[part(at)], gain_r1, 0, "seq", x, n_x, on_x)
    gain_r1[part(x)] = gain_part[part(x)]
    chunk_loop(0, normalize)
    chunk_loop(1, normalize)

    store_out = pltpu.make_async_copy(out_ref, out_hbm.at[0], store_sem.at[0])
    store_out.start()

    def grads(h):
        c = cols(h)
        grad = ga_ref[:, c]
        gs = jnp.where(causal, dot(grad, v_ref[:, c], 1, 1), 0.0).astype(BF16)
        query = dot(gs, k_ref[:, c], 1, 0) + dot(grad, ahead.result[c, :], 1, 1)
        gq_ref[:, c] = (scaling * query).astype(BF16)
        gk_part[:, c] = scaling * dot(gs, q_ref[:, c], 0, 0)
        gv_part[:, c] = dot(score_ref[c, :], grad, 0, 0)

    chunk_loop(0, grads)
    behind.relay(0)
    behind.relay(1)

    first.wait_recv()
    total = added(gain_r1, n_x)
    gain_s2[...] = total
    gain_r2[part(z)] = total
    second = gain_round(lambda at: gain_s2, gain_r2, 1, "seq", z, RING, lambda at: x * RING + at)

    chunk_loop(1, grads)
    store_gq = pltpu.make_async_copy(gq_ref, gq_hbm.at[0], store_sem.at[1])
    store_gq.start()

    behind.own(0)

    second.wait_recv()
    total = added(gain_r2, RING)
    gain_s3[...] = total
    gain_r3[part(dp)] = total
    third = gain_round(lambda at: gain_s3, gain_r3, 2, "dp", dp, n_dp, lambda at: at)

    behind.own(1)
    behind.give_near(0)
    behind.give_near(1)
    behind.pass_on(0)
    behind.pass_on(1)

    third.wait_recv()
    gain_r4[part(x)] = added(gain_r3, n_dp) / n_dp
    fourth = gain_round(lambda at: gain_r4.at[part(x)], gain_r4, 3, "seq", x, n_x, on_x)

    def finish(h):
        c = cols(h)
        suffix = behind.result[c, :]
        gk_ref[:, c] = (gk_part[:, c] + dot(v_ref[:, c], suffix, 1, 1)).astype(BF16)
        gv_ref[:, c] = (gv_part[:, c] + dot(k_ref[:, c], suffix, 1, 0)).astype(BF16)

    def put(h):
        c = cols(h)
        pltpu.make_async_copy(gk_ref.at[:, c], gk_hbm.at[0, :, c], store_sem.at[2]).start()
        pltpu.make_async_copy(gv_ref.at[:, c], gv_hbm.at[0, :, c], store_sem.at[3]).start()

    for chunk in range(CHUNKS):
        behind.arrive(chunk)
        chunk_loop(chunk, finish)
        chunk_loop(chunk, put)

    fourth.wait_recv()
    for h in range(HEADS):
        gain_out[h : h + 1, :] = gain_r4[h]
    store_gain = pltpu.make_async_copy(gain_out, gg_hbm, store_sem.at[4])
    store_gain.start()

    for chunk in range(CHUNKS):
        ahead.drain(chunk)
        behind.drain(chunk)
    first.wait_send()
    second.wait_send()
    third.wait_send()
    fourth.wait_send()
    store_gk = pltpu.make_async_copy(gk_ref, gk_hbm.at[0], store_sem.at[2])
    store_gv = pltpu.make_async_copy(gv_ref, gv_hbm.at[0], store_sem.at[3])
    for store in (store_out, store_gq, store_gk, store_gv, store_gain):
        store.wait()


def hand_out(*refs):
    sources, targets, sem = refs[:5], refs[5:10], refs[10]
    stores = [pltpu.make_async_copy(a, b, sem.at[i]) for i, (a, b) in enumerate(zip(sources, targets))]
    for store in stores:
        store.start()
    for store in stores:
        store.wait()


def stay(array):
    return pltpu.with_memory_space_constraint(array, pltpu.HBM)


def solution(mesh):
    n_seq = mesh.shape["seq"]
    n_dp = mesh.shape["dp"]

    def per_device(queries, keys, values, gain, cotangent):
        _, tokens, features = queries.shape
        grows = HEADS * RING // n_seq
        exact = pltpu.VMEM((tokens, features), F32)
        half = pltpu.VMEM((tokens, features), BF16)
        big = jax.ShapeDtypeStruct(queries.shape, BF16)
        anywhere = pl.BlockSpec(memory_space=pl.ANY)
        results = pl.pallas_call(
            functools.partial(kernel, n_seq, n_dp),
            out_shape=(big, big, big, big, jax.ShapeDtypeStruct((HEADS, HEAD), F32)),
            in_specs=[pl.BlockSpec(memory_space=pltpu.HBM)] * 5,
            out_specs=(anywhere,) * 5,
            scratch_shapes=[
                half,
                half,
                half,
                half,
                pltpu.VMEM((HEADS, HEAD), F32),
                exact,
                pltpu.VMEM((features, tokens), BF16),
                half,
                exact,
                exact,
                half,
                half,
                half,
                half,
            ]
            + pass_scratch(n_seq // RING) * 2
            + [
                pltpu.VMEM((HEADS, 1, HEAD), F32),
                pltpu.VMEM((HEADS, 1, HEAD), F32),
                pltpu.VMEM((grows, 1, HEAD), F32),
                pltpu.VMEM((RING * grows, 1, HEAD), F32),
                pltpu.VMEM((grows, 1, HEAD), F32),
                pltpu.VMEM((n_dp * grows, 1, HEAD), F32),
                pltpu.VMEM((HEADS, 1, HEAD), F32),
                pltpu.VMEM((HEADS, HEAD), F32),
                pltpu.SemaphoreType.DMA((7,)),
                pltpu.SemaphoreType.DMA((5,)),
                pltpu.SemaphoreType.DMA((2, CHUNKS, KINDS)),
                pltpu.SemaphoreType.DMA((2, CHUNKS, KINDS)),
                pltpu.SemaphoreType.DMA((4,)),
                pltpu.SemaphoreType.DMA((4,)),
            ],
            compiler_params=pltpu.CompilerParams(
                collective_id=0, has_side_effects=True, vmem_limit_bytes=32 * 2**20
            ),
        )(*(stay(a) for a in (queries, keys, values, gain.reshape(HEADS, HEAD), cotangent)))
        small = jax.ShapeDtypeStruct((HEADS, HEAD), F32)
        results = pl.pallas_call(
            hand_out,
            out_shape=(big, big, big, big, small),
            in_specs=[anywhere] * 5,
            out_specs=(anywhere,) * 5,
            scratch_shapes=[pltpu.SemaphoreType.DMA((5,))],
            compiler_params=pltpu.CompilerParams(vmem_limit_bytes=2**20),
        )(*results)
        return (*results[:4], results[4].reshape(features))

    sharded = P("dp", "seq", None)
    return jax.shard_map(
        per_device,
        mesh=mesh,
        in_specs=(sharded, sharded, sharded, P(), sharded),
        out_specs=(sharded, sharded, sharded, sharded, P()),
        check_vma=False,
    )
```

```python
import functools

import jax
import jax.numpy as jnp
from jax import lax
from jax.experimental import pallas as pl
from jax.experimental.pallas import tpu as pltpu
from jax.sharding import PartitionSpec as P

HEADS = 16
HEAD = 128
EPSILON = 1e-06
RING = 8
CHUNKS = 2
ENTRIES = 6
MESH = pl.DeviceIdType.MESH
F32 = jnp.float32
BF16 = jnp.bfloat16


def dot(a, b, ca, cb):
    return lax.dot_general(a, b, (((ca,), (cb,)), ((), ())), preferred_element_type=F32)


class ScanPass:
    def __init__(self, index, reverse, refs, send_sem, recv_sem, n_x):
        self.state, self.child, self.group, self.inbox, self.outbox, self.back, self.down, self.result = refs
        self.index, self.reverse, self.n_x = index, reverse, n_x
        self.send_sem, self.recv_sem = send_sem, recv_sem
        seq = lax.axis_index("seq")
        self.x, self.z = seq // RING, lax.rem(seq, RING)
        self.share = HEAD // n_x

    def ring(self, offset):
        return lax.rem(self.z + (offset + RING), RING)

    def rows(self, start, size):
        return pl.ds(pl.multiple_of(start, self.share), size)

    def head(self, c, k):
        return self.rows((k * RING + c) * HEAD, HEAD)

    def piece(self, c, k, x):
        return self.rows((k * RING + c) * HEAD + x * self.share, self.share)

    def spot(self, k, x, entry):
        return self.rows(((k * self.n_x + x) * ENTRIES + entry) * self.share, self.share)

    def tile(self, k, i, count):
        return self.rows((k * count + i) * HEAD, HEAD)

    def tile_part(self, k, i, count, x):
        return self.rows((k * count + i) * HEAD + x * self.share, self.share)

    def copy(self, src, dst, k, send, recv, x, z):
        return pltpu.make_async_remote_copy(
            src_ref=src,
            dst_ref=dst,
            send_sem=self.send_sem.at[self.index, k, send],
            recv_sem=self.recv_sem.at[self.index, k, recv],
            device_id={"seq": x * RING + z},
            device_id_type=MESH,
        )

    def taken(self, count, k, kind):
        part = pl.ds(0, count * self.share)
        return self.copy(self.state.at[part], self.result.at[part], k, kind, kind, self.x, self.ring(1))

    def odd(self):
        return jnp.logical_or(self.z == 0, self.z == RING - 1)

    def even_inner(self):
        return jnp.logical_and(self.z != 0, lax.rem(self.z, 2) == 0)

    def odd_inner(self):
        return jnp.logical_and(self.z != RING - 1, lax.rem(self.z, 2) == 1)

    def odd_owner(self):
        return jnp.logical_or(self.z == 2, self.z == 5)

    def odd_target(self):
        return jnp.where(self.z == 0, 5, 2)

    def clear(self):
        zero = jnp.zeros((HEAD, HEAD), BF16)
        few = jnp.zeros((self.share, HEAD), BF16)

        def blank(slot):
            for k in range(CHUNKS):
                self.child[self.tile(k, slot, 5), :] = zero

        pl.when(self.z == 0)(lambda: blank(0))
        pl.when(self.z == RING - 1)(lambda: blank(2))
        pl.when(jnp.logical_not(self.even_inner()))(lambda: blank(1))
        pl.when(jnp.logical_not(self.odd_inner()))(lambda: blank(3))

        @pl.when(jnp.logical_not(self.odd_owner()))
        def _():
            for k in range(CHUNKS):
                for x in range(self.n_x):
                    self.inbox[self.spot(k, x, 0), :] = few

    def send_far(self, k):
        z = self.z

        def hand(offset, to, slot, send):
            self.copy(
                self.state.at[self.head(self.ring(offset), k)],
                self.child.at[self.tile(k, slot, 5)],
                k,
                send,
                slot if slot < 4 else 13,
                self.x,
                to,
            ).start()

        even = lax.rem(z, 2) == 0
        pl.when(jnp.logical_and(even, z != 6))(lambda: hand(4, z + 2, 1, 2))
        pl.when(jnp.logical_not(jnp.logical_or(even, z == 1)))(lambda: hand(4, z - 2, 3, 2))
        pl.when(z == 6)(lambda: hand(4, z + 1, 4, 2))
        pl.when(z == 1)(lambda: hand(4, z - 1, 4, 2))
        pl.when(z != RING - 1)(lambda: hand(3, z + 1, 0, 0))
        pl.when(z != 0)(lambda: hand(-3, z - 1, 2, 1))

    def send_near(self, k):
        z, n_x = self.z, self.n_x

        def direct(c, x, entry, kind):
            self.copy(
                self.state.at[self.piece(c, k, x)], self.inbox.at[self.spot(k, self.x, entry)], k, kind, kind, x, c
            ).start()

        for i in range(n_x):
            x = lax.rem(self.x + (i + 1), n_x)
            direct(self.ring(1), x, 2, 4)
            direct(self.ring(-1), x, 4, 4)
            if i < n_x - 1:
                direct(z, x, 3, 4)
        self.inbox[self.spot(k, self.x, 3), :] = self.state[self.piece(z, k, self.x), :]

    def relay(self, k):
        z, n_x = self.z, self.n_x
        whole = n_x
        for side in range(2):
            if side == 0:
                pl.when(z != 0)(lambda: self.taken(whole, k, 0).wait_recv())
                pl.when(self.even_inner())(lambda: self.taken(whole, k, 1).wait_recv())
            else:
                pl.when(z != RING - 1)(lambda: self.taken(whole, k, 2).wait_recv())
                pl.when(self.odd_inner())(lambda: self.taken(whole, k, 3).wait_recv())
            c = self.ring(2 - 4 * side)
            total = self.state[self.head(c, k), :].astype(F32)
            total = total + self.child[self.tile(k, 2 * side, 5), :].astype(F32)
            total = total + self.child[self.tile(k, 2 * side + 1, 5), :].astype(F32)
            self.group[self.tile(k, side, 3), :] = total.astype(BF16)
            for i in range(n_x):
                x = lax.rem(self.x + (i + 1), n_x)
                self.copy(
                    self.group.at[self.tile_part(k, side, 3, x)],
                    self.inbox.at[self.spot(k, self.x, 1 + 4 * side)],
                    k,
                    4,
                    4,
                    x,
                    c,
                ).start()

        @pl.when(self.odd())
        def _():
            self.taken(whole, k, 13).wait_recv()
            c = self.odd_target()
            total = self.state[self.head(c, k), :].astype(F32) + self.child[self.tile(k, 4, 5), :].astype(F32)
            self.group[self.tile(k, 2, 3), :] = total.astype(BF16)
            for i in range(n_x):
                x = lax.rem(self.x + (i + 1), n_x)
                source = self.group.at[self.tile_part(k, 2, 3, x)]
                self.copy(source, self.inbox.at[self.spot(k, self.x, 0)], k, 5, 5, x, c).start()

    def own(self, k):
        z, n_x = self.z, self.n_x
        pl.when(self.odd_owner())(lambda: self.taken(n_x, k, 5).wait_recv())
        self.taken(5 * n_x - 1, k, 4).wait_recv()
        first = jnp.where(z <= 3, 3 - z, jnp.where(z <= 5, 0, 11 - z))
        total = jnp.zeros((self.share, HEAD), F32)
        for i in range(n_x * ENTRIES):
            j = n_x * ENTRIES - 1 - i if self.reverse else i
            spot = self.spot(k, j // ENTRIES, lax.rem(first + j % ENTRIES, ENTRIES))
            self.outbox[spot, :] = total.astype(BF16)
            total = total + self.inbox[spot, :].astype(F32)

        def give_group(x, side):
            self.copy(
                self.outbox.at[self.spot(k, x, 1 + 4 * side)],
                self.back.at[self.tile_part(k, side, 3, self.x)],
                k,
                6,
                8 + side,
                x,
                self.ring(4 * side - 2),
            ).start()

        for i in range(n_x):
            x = lax.rem(self.x + (i + 1), n_x)
            give_group(x, 0)
            give_group(x, 1)

        @pl.when(self.odd_owner())
        def _():
            for i in range(n_x):
                x = lax.rem(self.x + (i + 1), n_x)
                target = self.back.at[self.tile_part(k, 2, 3, self.x)]
                to = jnp.where(z == 2, RING - 1, 0)
                self.copy(self.outbox.at[self.spot(k, x, 0)], target, k, 7, 7, x, to).start()

    def give_near(self, k):
        z, n_x = self.z, self.n_x

        def give(x, to, entry, kind):
            self.copy(
                self.outbox.at[self.spot(k, x, entry)], self.result.at[self.piece(z, k, self.x)], k, kind, kind, x, to
            ).start()

        for i in range(n_x):
            x = lax.rem(self.x + (i + 1), n_x)
            give(x, self.ring(-1), 2, 6)
            give(x, self.ring(1), 4, 6)
            if i < n_x - 1:
                give(x, z, 3, 6)
        self.result[self.piece(z, k, self.x), :] = self.outbox[self.spot(k, self.x, 3), :]

    def pass_on(self, k):
        z = self.z
        for side in range(2):
            c = self.ring(2 - 4 * side)
            self.taken(self.n_x, k, 8 + side).wait_recv()
            base = self.back[self.tile(k, side, 3), :].astype(F32)
            mine = self.state[self.head(c, k), :].astype(F32)
            near = self.child[self.tile(k, 2 * side, 5), :].astype(F32)
            far = self.child[self.tile(k, 2 * side + 1, 5), :].astype(F32)
            if (side == 0) != self.reverse:
                for_far = base
                for_near = base + far
                for_mine = for_near + near
            else:
                for_mine = base
                for_near = base + mine
                for_far = for_near + near
            self.down[self.tile(k, 2 * side + 1, 5), :] = for_far.astype(BF16)
            self.down[self.tile(k, 2 * side, 5), :] = for_near.astype(BF16)
            self.result[self.head(c, k), :] = for_mine.astype(BF16)

        def hand(side, slot, to, send, recv):
            self.copy(
                self.down.at[self.tile(k, slot, 5)],
                self.result.at[self.head(self.ring(2 - 4 * side), k)],
                k,
                send,
                recv,
                self.x,
                to,
            ).start()

        pl.when(self.even_inner())(lambda: hand(0, 1, z - 2, 10, 12))
        pl.when(self.odd_inner())(lambda: hand(1, 3, z + 2, 10, 12))
        pl.when(z != 0)(lambda: hand(0, 0, z - 1, 8, 10))
        pl.when(z != RING - 1)(lambda: hand(1, 2, z + 1, 9, 11))

        @pl.when(self.odd())
        def _():
            self.taken(self.n_x, k, 7).wait_recv()
            c = self.odd_target()
            base = self.back[self.tile(k, 2, 3), :].astype(F32)
            mine = base + self.child[self.tile(k, 4, 5), :].astype(F32)
            theirs = base + self.state[self.head(c, k), :].astype(F32)
            their_turn = (z == RING - 1) != self.reverse
            self.down[self.tile(k, 4, 5), :] = jnp.where(their_turn, base, theirs).astype(BF16)
            self.result[self.head(c, k), :] = jnp.where(their_turn, mine, base).astype(BF16)
            to = jnp.where(z == 0, 1, RING - 2)
            self.copy(
                self.down.at[self.tile(k, 4, 5)], self.result.at[self.head(c, k)], k, 10, 12, self.x, to
            ).start()

    def arrive(self, k):
        z, n_x = self.z, self.n_x
        self.taken(3 * n_x - 1, k, 6).wait_recv()
        pl.when(z != RING - 1)(lambda: self.taken(n_x, k, 10).wait_recv())
        pl.when(z != 0)(lambda: self.taken(n_x, k, 11).wait_recv())
        self.taken(n_x, k, 12).wait_recv()

    def drain(self, k):
        z, n_x = self.z, self.n_x

        def sent(count, kind):
            self.taken(count, k, kind).wait_send()

        pl.when(z != RING - 1)(lambda: sent(n_x, 0))
        pl.when(z != 0)(lambda: sent(n_x, 1))
        sent(n_x, 2)
        sent(5 * n_x - 1, 4)
        pl.when(self.odd())(lambda: sent(n_x, 5))
        sent(5 * n_x - 1, 6)
        pl.when(self.odd_owner())(lambda: sent(n_x, 7))
        pl.when(z != 0)(lambda: sent(n_x, 8))
        pl.when(z != RING - 1)(lambda: sent(n_x, 9))
        sent(n_x, 10)


PASS_REFS = 8
KINDS = 14


def pass_scratch(n_x):
    tiles = CHUNKS * HEAD
    sizes = (
        HEADS * HEAD,
        5 * tiles,
        3 * tiles,
        ENTRIES * tiles,
        ENTRIES * tiles,
        3 * tiles,
        5 * tiles,
        HEADS * HEAD,
    )
    return [pltpu.VMEM((size, HEAD), BF16) for size in sizes]


def chunk_loop(k, body):
    @pl.loop(0, RING // 4)
    def _(step):
        for inner in range(4):
            body(k * RING + step * 4 + inner)


def kernel(
    n_seq,
    n_dp,
    q_hbm,
    k_hbm,
    v_hbm,
    gain_hbm,
    cot_hbm,
    out_hbm,
    gq_hbm,
    gk_hbm,
    gv_hbm,
    gg_hbm,
    q_ref,
    k_ref,
    v_ref,
    cot_ref,
    gain_ref,
    att_ref,
    score_ref,
    ga_ref,
    gk_part,
    gv_part,
    out_ref,
    gq_ref,
    gk_ref,
    gv_ref,
    *rest,
):
    ahead_refs, rest = rest[:PASS_REFS], rest[PASS_REFS:]
    behind_refs, rest = rest[:PASS_REFS], rest[PASS_REFS:]
    gain_part, gain_r1, gain_s2, gain_r2, gain_s3, gain_r3, gain_r4, gain_out, *sems = rest
    load_sem, store_sem, send_sem, recv_sem, gain_send_sem, gain_recv_sem = sems
    seq = lax.axis_index("seq")
    dp = lax.axis_index("dp")
    n_x = n_seq // RING
    ahead = ScanPass(0, False, ahead_refs, send_sem, recv_sem, n_x)
    behind = ScanPass(1, True, behind_refs, send_sem, recv_sem, n_x)
    tokens = q_ref.shape[0]
    features = HEADS * HEAD
    scaling = HEAD ** (-0.5)
    grows = HEADS // n_x

    def cols(h):
        return pl.ds(pl.multiple_of(h * HEAD, HEAD), HEAD)

    half = features // CHUNKS
    early = []
    for k in range(CHUNKS):
        for i, (src, dst) in enumerate(((k_hbm, k_ref), (v_hbm, v_ref))):
            part_of = pl.ds(k * half, half)
            early.append(
                pltpu.make_async_copy(src.at[0, :, part_of], dst.at[:, part_of], load_sem.at[CHUNKS * k + i])
            )
    loads = [
        pltpu.make_async_copy(q_hbm.at[0], q_ref, load_sem.at[4]),
        pltpu.make_async_copy(cot_hbm.at[0], cot_ref, load_sem.at[5]),
        pltpu.make_async_copy(gain_hbm, gain_ref, load_sem.at[6]),
    ]
    for load in early + loads:
        load.start()

    barrier = pltpu.get_barrier_semaphore()

    for step in range(n_x):
        for offset in (1, -1, 2, -2, 0, 3, -3, 4):
            if step == 0 and offset == 0:
                continue
            peer = lax.rem(ahead.x + step, n_x) * RING + ahead.ring(offset)
            pl.semaphore_signal(barrier, inc=1, device_id={"seq": peer}, device_id_type=MESH)

    @pl.loop(1, n_dp)
    def _(k):
        peer = lax.rem(dp + k, n_dp)
        pl.semaphore_signal(barrier, inc=1, device_id={"dp": peer}, device_id_type=MESH)

    ahead.clear()
    behind.clear()

    position_t = lax.broadcasted_iota(jnp.int32, (tokens, tokens), 0)
    position_u = lax.broadcasted_iota(jnp.int32, (tokens, tokens), 1)
    causal = position_t >= position_u

    def state_of(h):
        c = cols(h)
        ahead.state[c, :] = dot(k_ref[:, c], v_ref[:, c], 0, 0).astype(BF16)

    early[0].wait()
    early[1].wait()
    chunk_loop(0, state_of)
    pl.semaphore_wait(barrier, n_seq - 1 + n_dp - 1)
    ahead.send_far(0)
    early[2].wait()
    early[3].wait()
    chunk_loop(1, state_of)
    ahead.send_far(1)
    ahead.send_near(0)
    ahead.send_near(1)

    for load in loads:
        load.wait()

    def local_of(h):
        c = cols(h)
        raw = dot(q_ref[:, c], k_ref[:, c], 1, 1)
        score = jnp.where(causal, raw * scaling, 0.0).astype(BF16)
        score_ref[c, :] = score
        att_ref[:, c] = dot(score, v_ref[:, c], 1, 0)

    chunk_loop(0, local_of)
    ahead.relay(0)
    ahead.relay(1)
    chunk_loop(1, local_of)
    ahead.own(0)
    ahead.give_near(0)
    ahead.own(1)
    ahead.give_near(1)
    ahead.pass_on(0)
    ahead.pass_on(1)

    def attend(chunk, step, carry):
        squares, inner = carry
        for k in range(4):
            h = chunk * RING + step * 4 + k
            c = cols(h)
            att = att_ref[:, c] + scaling * dot(q_ref[:, c], ahead.result[c, :], 1, 0)
            att_ref[:, c] = att
            squares = squares + att * att
            inner = inner + att * (cot_ref[:, c].astype(F32) * gain_ref[pl.ds(h, 1), :])
        return squares, inner

    zero = jnp.zeros((tokens, HEAD), F32)
    carry = (zero, zero)
    for chunk in range(CHUNKS):
        ahead.arrive(chunk)
        carry = lax.fori_loop(0, RING // 4, functools.partial(attend, chunk), carry)
    squares, inner = carry
    root = jnp.sqrt(jnp.sum(squares, axis=1, keepdims=True) / features + EPSILON)
    inverse = 1.0 / root
    mean = jnp.sum(inner, axis=1, keepdims=True) * inverse / features

    def pull(h):
        c = cols(h)
        upstream = cot_ref[:, c].astype(F32)
        normalized = att_ref[:, c] * inverse
        grad = ((upstream * gain_ref[pl.ds(h, 1), :] - normalized * mean) * inverse).astype(BF16)
        ga_ref[:, c] = grad
        behind.state[c, :] = (scaling * dot(q_ref[:, c], grad, 0, 0)).astype(BF16)

    def normalize(h):
        c = cols(h)
        normalized = att_ref[:, c] * inverse
        out_ref[:, c] = (gain_ref[pl.ds(h, 1), :] * normalized).astype(BF16)

    def gain_of(h):
        c = cols(h)
        gain_part[h] = jnp.sum(cot_ref[:, c].astype(F32) * (att_ref[:, c] * inverse), axis=0, keepdims=True)

    x, z = seq // RING, lax.rem(seq, RING)

    def gain_copy(src, dst, index, axis, peer):
        return pltpu.make_async_remote_copy(
            src_ref=src,
            dst_ref=dst,
            send_sem=gain_send_sem.at[index],
            recv_sem=gain_recv_sem.at[index],
            device_id={axis: peer},
            device_id_type=MESH,
        )

    def part(j):
        return pl.ds(j * grows, grows)

    def added(parts, count):
        total = parts[part(0)]
        for j in range(1, count):
            total = total + parts[part(j)]
        return total

    def gain_round(src_of, dst, index, axis, me, count, peer_of):
        @pl.loop(1, count)
        def _(k):
            at = lax.rem(me + k, count)
            gain_copy(src_of(at), dst.at[part(me)], index, axis, peer_of(at)).start()

        rest = pl.ds(0, (count - 1) * grows)
        return gain_copy(dst.at[rest], dst.at[rest], index, axis, peer_of(lax.rem(me + 1, count)))

    def on_x(at):
        return at * RING + z

    chunk_loop(0, pull)
    behind.send_far(0)
    chunk_loop(1, pull)
    behind.send_far(1)
    chunk_loop(0, gain_of)
    chunk_loop(1, gain_of)
    behind.send_near(0)
    behind.send_near(1)
    first = gain_round(lambda at: gain_part.at[part(at)], gain_r1, 0, "seq", x, n_x, on_x)
    gain_r1[part(x)] = gain_part[part(x)]
    chunk_loop(0, normalize)
    chunk_loop(1, normalize)

    store_out = pltpu.make_async_copy(out_ref, out_hbm.at[0], store_sem.at[0])
    store_out.start()

    def grads(h):
        c = cols(h)
        grad = ga_ref[:, c]
        gs = jnp.where(causal, dot(grad, v_ref[:, c], 1, 1), 0.0).astype(BF16)
        query = dot(gs, k_ref[:, c], 1, 0) + dot(grad, ahead.result[c, :], 1, 1)
        gq_ref[:, c] = (scaling * query).astype(BF16)
        gk_part[:, c] = scaling * dot(gs, q_ref[:, c], 0, 0)
        gv_part[:, c] = dot(score_ref[c, :], grad, 0, 0)

    chunk_loop(0, grads)
    behind.relay(0)
    behind.relay(1)

    first.wait_recv()
    total = added(gain_r1, n_x)
    gain_s2[...] = total
    gain_r2[part(z)] = total
    second = gain_round(lambda at: gain_s2, gain_r2, 1, "seq", z, RING, lambda at: x * RING + at)

    chunk_loop(1, grads)
    store_gq = pltpu.make_async_copy(gq_ref, gq_hbm.at[0], store_sem.at[1])
    store_gq.start()

    behind.own(0)
    behind.give_near(0)

    second.wait_recv()
    total = added(gain_r2, RING)
    gain_s3[...] = total
    gain_r3[part(dp)] = total
    third = gain_round(lambda at: gain_s3, gain_r3, 2, "dp", dp, n_dp, lambda at: at)

    behind.own(1)
    behind.give_near(1)
    behind.pass_on(0)
    behind.pass_on(1)

    third.wait_recv()
    gain_r4[part(x)] = added(gain_r3, n_dp) / n_dp
    fourth = gain_round(lambda at: gain_r4.at[part(x)], gain_r4, 3, "seq", x, n_x, on_x)

    def finish(h):
        c = cols(h)
        suffix = behind.result[c, :]
        gk_ref[:, c] = (gk_part[:, c] + dot(v_ref[:, c], suffix, 1, 1)).astype(BF16)
        gv_ref[:, c] = (gv_part[:, c] + dot(k_ref[:, c], suffix, 1, 0)).astype(BF16)

    def put(h):
        c = cols(h)
        pltpu.make_async_copy(gk_ref.at[:, c], gk_hbm.at[0, :, c], store_sem.at[2]).start()
        pltpu.make_async_copy(gv_ref.at[:, c], gv_hbm.at[0, :, c], store_sem.at[3]).start()

    for chunk in range(CHUNKS):
        behind.arrive(chunk)
        chunk_loop(chunk, finish)
        chunk_loop(chunk, put)

    fourth.wait_recv()
    for h in range(HEADS):
        gain_out[h : h + 1, :] = gain_r4[h]
    store_gain = pltpu.make_async_copy(gain_out, gg_hbm, store_sem.at[4])
    store_gain.start()

    for chunk in range(CHUNKS):
        ahead.drain(chunk)
        behind.drain(chunk)
    first.wait_send()
    second.wait_send()
    third.wait_send()
    fourth.wait_send()
    store_gk = pltpu.make_async_copy(gk_ref, gk_hbm.at[0], store_sem.at[2])
    store_gv = pltpu.make_async_copy(gv_ref, gv_hbm.at[0], store_sem.at[3])
    for store in (store_out, store_gq, store_gk, store_gv, store_gain):
        store.wait()


def hand_out(*refs):
    sources, targets, sem = refs[:5], refs[5:10], refs[10]
    stores = [pltpu.make_async_copy(a, b, sem.at[i]) for i, (a, b) in enumerate(zip(sources, targets))]
    for store in stores:
        store.start()
    for store in stores:
        store.wait()


def stay(array):
    return pltpu.with_memory_space_constraint(array, pltpu.HBM)


def solution(mesh):
    n_seq = mesh.shape["seq"]
    n_dp = mesh.shape["dp"]

    def per_device(queries, keys, values, gain, cotangent):
        _, tokens, features = queries.shape
        grows = HEADS * RING // n_seq
        exact = pltpu.VMEM((tokens, features), F32)
        half = pltpu.VMEM((tokens, features), BF16)
        big = jax.ShapeDtypeStruct(queries.shape, BF16)
        anywhere = pl.BlockSpec(memory_space=pl.ANY)
        results = pl.pallas_call(
            functools.partial(kernel, n_seq, n_dp),
            out_shape=(big, big, big, big, jax.ShapeDtypeStruct((HEADS, HEAD), F32)),
            in_specs=[pl.BlockSpec(memory_space=pltpu.HBM)] * 5,
            out_specs=(anywhere,) * 5,
            scratch_shapes=[
                half,
                half,
                half,
                half,
                pltpu.VMEM((HEADS, HEAD), F32),
                exact,
                pltpu.VMEM((features, tokens), BF16),
                half,
                exact,
                exact,
                half,
                half,
                half,
                half,
            ]
            + pass_scratch(n_seq // RING) * 2
            + [
                pltpu.VMEM((HEADS, 1, HEAD), F32),
                pltpu.VMEM((HEADS, 1, HEAD), F32),
                pltpu.VMEM((grows, 1, HEAD), F32),
                pltpu.VMEM((RING * grows, 1, HEAD), F32),
                pltpu.VMEM((grows, 1, HEAD), F32),
                pltpu.VMEM((n_dp * grows, 1, HEAD), F32),
                pltpu.VMEM((HEADS, 1, HEAD), F32),
                pltpu.VMEM((HEADS, HEAD), F32),
                pltpu.SemaphoreType.DMA((7,)),
                pltpu.SemaphoreType.DMA((5,)),
                pltpu.SemaphoreType.DMA((2, CHUNKS, KINDS)),
                pltpu.SemaphoreType.DMA((2, CHUNKS, KINDS)),
                pltpu.SemaphoreType.DMA((4,)),
                pltpu.SemaphoreType.DMA((4,)),
            ],
            compiler_params=pltpu.CompilerParams(
                collective_id=0, has_side_effects=True, vmem_limit_bytes=32 * 2**20
            ),
        )(*(stay(a) for a in (queries, keys, values, gain.reshape(HEADS, HEAD), cotangent)))
        small = jax.ShapeDtypeStruct((HEADS, HEAD), F32)
        results = pl.pallas_call(
            hand_out,
            out_shape=(big, big, big, big, small),
            in_specs=[anywhere] * 5,
            out_specs=(anywhere,) * 5,
            scratch_shapes=[pltpu.SemaphoreType.DMA((5,))],
            compiler_params=pltpu.CompilerParams(vmem_limit_bytes=2**20),
        )(*results)
        return (*results[:4], results[4].reshape(features))

    sharded = P("dp", "seq", None)
    return jax.shard_map(
        per_device,
        mesh=mesh,
        in_specs=(sharded, sharded, sharded, P(), sharded),
        out_specs=(sharded, sharded, sharded, sharded, P()),
        check_vma=False,
    )
```
